32 devices in a mesh: gx: 8 (over z, x), gy: 4 (over y, core).
Axes of the slice: x: 2, y: 2, z: 4, core: 2. Of those that a mesh axis runs over, the one named last changes fastest.
Arguments:
- ensemble: float32 [16, 512, 1024], P('gx', None, 'gy'), may hold values from -6 to 6
- obs_values: float32 [4, 128], replicated, may hold values from -6 to 6
- obs_error: float32 [4, 128], replicated, may hold values from 0.3 to 3
- tile_weight: float32 [4, 128, 8, 4], P(None, None, 'gx', 'gy'), may hold values from 0.2 to 1
- owner_device: int32 [4], replicated, may hold values from 0 to 31
- obs_cells: int32 [4, 128], replicated, may hold values from 0 to 16383
Outputs:
- analysis_ensemble: float32 [16, 512, 1024], P('gx', None, 'gy')
The draws below stay inside these ranges and needn't reach their ends.
Inputs may be any that keep to these rules, and one draw needn't show every extreme that they name: `owner_device`: device numbers count gy fastest: the device at index i of gx and j of gy is number i times the length of gy plus j. `obs_cells`: cell c of a tile lies c // 256 cells along the first direction and c % 256 along the second from the tile's first cell; cells may repeat.
All inputs are finite; a program needn't handle non-finite values.
Results may differ from the reference program's by a relative error of at most 0.00015.
Values sent between devices are 32-bit elements; how exact they have to be, the bound alone decides.
No kernel may reach another device: no remote copies, remote signals or barrier semaphores. Data moves between devices by JAX's collectives and lax.ppermute only.
A program may use at most 64 MiB of HBM per device.

```python
import math
import jax
import jax.numpy as jnp
from jax import lax

VX = 64
VY = 256
NB = 4
NOBS = 128
MEMBERS = 16
NVX = 512
NVY = 1024
REACH = 128
N_GX = 8
N_GY = 4


def touch_ends(values, stream_key, smallest, high):
    index_at = [jax.random.randint(jax.random.fold_in(stream_key, axis), (), 0, length) for axis, length in enumerate(values.shape)]
    longest = values.shape.index(max(values.shape))
    neighbour = index_at[:longest] + [(index_at[longest] + 1) % values.shape[longest]] + index_at[longest + 1:]
    return values.at[tuple(index_at)].set(smallest).at[tuple(neighbour)].set(high)


def block_scale(stream_key, shape, pieces, low, high):
    gain, own = 1.0, jax.random.fold_in(stream_key, 6)
    for axis_at, blocks in pieces:
        draws = jnp.exp(jax.random.uniform(jax.random.fold_in(own, axis_at), (blocks,), jnp.float32, low / len(pieces), high / len(pieces)))
        gain = gain * jnp.repeat(draws, shape[axis_at] // blocks).reshape([-1 if axis == axis_at else 1 for axis in range(len(shape))])
    return gain


def normal_values(key, extent, scale, limit, cuts=(), kind=jnp.bfloat16):
    array = scale * jax.random.normal(key, extent, jnp.float32)
    if cuts:
        array = array * block_scale(key, extent, cuts, -0.22, 0.18)
    return jnp.clip(array, -limit, limit).astype(kind)


def setup_inputs(seed: int = 0) -> dict:
    splits = jax.random.split(jax.random.key(seed), 7)
    return {
        "ensemble": normal_values(splits[0], (MEMBERS, NVX, NVY), 1.0, 6.0, ((0, 8), (2, 4)), jnp.float32),
        "obs_values": normal_values(splits[1], (NB, NOBS), 1.0, 6.0, (), jnp.float32),
        "obs_error": jnp.clip(jnp.exp(jax.random.uniform(splits[2], (NB, NOBS), jnp.float32, math.log(0.3), math.log(3.0))), 0.3, 3.0),
        "tile_weight": jnp.clip(0.2 + 0.8 * jax.random.uniform(splits[3], (NB, NOBS, N_GX, N_GY), jnp.float32) ** block_scale(splits[3], (NB, NOBS, N_GX, N_GY), ((2, 8), (3, 4)), -0.2, 0.2), 0.2, 1.0),
        "owner_device": touch_ends(jax.random.randint(splits[4], (NB,), 0, N_GX * N_GY), jax.random.fold_in(splits[4], 1), 0, (N_GX * N_GY) - 1).astype(jnp.int32),
        "obs_cells": touch_ends(jax.random.randint(splits[5], (NB, NOBS), 0, VX * VY), jax.random.fold_in(splits[5], 1), 0, (VX * VY) - 1).astype(jnp.int32),
    }


EPSILON = 1e-06
PRECISE = lax.Precision.HIGHEST

def analysis(prior_ens, values, errors):
    members = prior_ens.shape[1]
    average = lax.optimization_barrier(jnp.mean(prior_ens, axis=1, keepdims=True))
    anomaly = prior_ens - average
    spread = lax.optimization_barrier(jnp.sum(anomaly * anomaly, axis=1, keepdims=True)) / (members - 1) + EPSILON
    obs_noise = errors[:, None]
    post_var = 1.0 / (1.0 / spread + 1.0 / obs_noise)
    post_mean = post_var * (average / spread + values[:, None] / obs_noise)
    increment = post_mean - average + (jnp.sqrt(post_var / spread) - 1.0) * anomaly
    return (anomaly, spread, increment)

def regression(state_cols, anomaly, spread, increment, weight_cols, obs_xpos, obs_ypos, grid_xpos, grid_ypos, radius):
    members = state_cols.shape[0]
    deviation = state_cols - lax.optimization_barrier(jnp.mean(state_cols, axis=0, keepdims=True))
    covariance = jnp.dot(anomaly, deviation, precision=PRECISE) / (members - 1)
    distance = (grid_xpos[None, :] - obs_xpos[:, None]) ** 2 + (grid_ypos[None, :] - obs_ypos[:, None]) ** 2
    tapering = 1.0 / (1.0 + distance / radius)
    gain_rows = covariance * (tapering * weight_cols) / spread
    return state_cols + jnp.dot(increment.T, gain_rows, precision=PRECISE)

def reference(ensemble, obs_values, obs_error, tile_weight, owner_device, obs_cells):
    current = ensemble
    radius = float(REACH * REACH)
    cell_ids = jnp.arange(VX * NVY, dtype=jnp.int32)
    for batch in range(NB):
        owner_now = owner_device[batch]
        observed = obs_cells[batch]
        obs_gridx = owner_now // N_GY * VX + observed // VY
        obs_gridy = owner_now % N_GY * VY + observed % VY
        prior_ens = current[:, obs_gridx, obs_gridy].T
        anomaly, spread, increment = analysis(prior_ens, obs_values[batch], obs_error[batch])
        obs_xpos = obs_gridx.astype(jnp.float32)
        obs_ypos = obs_gridy.astype(jnp.float32)
        weights = tile_weight[batch]
        blocks = current.reshape(MEMBERS, N_GX, VX, NVY).transpose(1, 0, 2, 3)

        def update_block(element):
            x_block, column = element
            grid_xpos = (column * VX + cell_ids // NVY).astype(jnp.float32)
            grid_ypos = (cell_ids % NVY).astype(jnp.float32)
            stripe = jnp.repeat(weights[:, column, :], VY, axis=1)
            weight_cols = jnp.tile(stripe, (1, VX))
            state_cols = x_block.reshape(MEMBERS, VX * NVY)
            updated = regression(state_cols, anomaly, spread, increment, weight_cols, obs_xpos, obs_ypos, grid_xpos, grid_ypos, radius)
            return updated.reshape(MEMBERS, VX, NVY)
        updated = lax.map(update_block, (blocks, jnp.arange(N_GX, dtype=jnp.int32)))
        current = updated.transpose(1, 0, 2, 3).reshape(MEMBERS, NVX, NVY)
    return current
```

```python
import functools

import jax
import jax.numpy as jnp
from jax import lax
from jax.experimental import pallas as pl
from jax.experimental.pallas import tpu as pltpu
from jax.sharding import PartitionSpec as P

EPSILON = 1e-06
CHUNKS = 1
ROWS = 8
F32 = jnp.float32
BF16 = jnp.bfloat16
VMEM = pltpu.MemorySpace.VMEM
SMEM = pltpu.MemorySpace.SMEM


def split_two(value):
    high = value.astype(BF16)
    low = (value - high.astype(F32)).astype(BF16)
    return high, low


def pairs_of(batches):
    return [(b, later) for b in range(batches) for later in range(b + 1, batches)]


def pick_body(owner_ref, cells_ref, weight_ref, ens_ref, out_ref, window, sems, *, tile_rows, gy_count):
    batches, nobs = cells_ref.shape
    held, _, cols = ens_ref.shape
    row_at = lax.axis_index("gx")
    col_at = lax.axis_index("gy")
    me = row_at * gy_count + col_at

    def fetch(b):
        first = pl.multiple_of((owner_ref[b] // gy_count) * tile_rows, tile_rows)
        return pltpu.make_async_copy(
            ens_ref.at[:, pl.ds(first, tile_rows), :], window.at[b], sems.at[b]
        )

    for b in range(batches):
        fetch(b).start()
    out_ref[...] = jnp.zeros_like(out_ref)
    for at, (b, later) in enumerate(pairs_of(batches)):
        row = held * batches + at
        out_ref[row : row + 1, :] = jnp.where(owner_ref[later] == me, weight_ref[b : b + 1, :], 0.0)
    for b in range(batches):
        fetch(b).wait()
        cell = cells_ref[b : b + 1, :]
        row_hit = (lax.broadcasted_iota(jnp.int32, (tile_rows, nobs), 0) == cell // cols).astype(F32)
        row_hit = row_hit.astype(BF16)
        row_hit = jnp.concatenate([row_hit] * 3, axis=0)
        col_hit = lax.broadcasted_iota(jnp.int32, (cols, nobs), 0) == cell % cols
        mine = owner_ref[b] % gy_count == col_at
        for m in range(held):
            values = window[b, m]
            high = values.astype(BF16)
            rest = values - high.astype(F32)
            middle, low = split_two(rest)
            stacked = jnp.concatenate([high, middle, low], axis=0)
            columns = lax.dot_general(
                stacked, row_hit, (((0,), (0,)), ((), ())), preferred_element_type=F32
            )
            picked = jnp.sum(jnp.where(col_hit, columns, 0.0), axis=0, keepdims=True)
            row = m * batches + b
            out_ref[row : row + 1, :] = jnp.where(mine, picked, 0.0)


def chain_body(
    owner_ref,
    cells_ref,
    values_ref,
    errors_ref,
    weight_ref,
    got_ref,
    a_ref,
    w_ref,
    x_ref,
    y_ref,
    prior_ref,
    *,
    tile_rows,
    tile_cols,
    held,
    gx_count,
    gy_count,
    inverse,
):
    batches, nobs = cells_ref.shape
    members = held * gx_count
    col_at = lax.axis_index("gy")
    payload = got_ref.shape[1]
    weights = jnp.zeros((payload, nobs), F32)
    for g in range(gx_count):
        part = got_ref[g * gy_count]
        for j in range(1, gy_count):
            part = part + got_ref[g * gy_count + j]
        weights = weights + part
        for m in range(held):
            for b in range(batches):
                row = m * batches + b
                prior_ref[b, held * g + m : held * g + m + 1, :] = part[row : row + 1, :]
    pair_weight = {
        pair: weights[held * batches + at : held * batches + at + 1, :]
        for at, pair in enumerate(pairs_of(batches))
    }
    rows_x, rows_y, cols_x, cols_y = [], [], [], []
    for b in range(batches):
        cell = cells_ref[b : b + 1, :]
        owner = owner_ref[b]
        ox = ((owner // gy_count) * tile_rows + cell // tile_cols).astype(F32) * inverse
        oy = ((owner % gy_count) * tile_cols + cell % tile_cols).astype(F32) * inverse
        rows_x.append(ox)
        rows_y.append(oy)
        cols_x.append(jnp.transpose(jnp.broadcast_to(ox, (nobs, nobs))))
        cols_y.append(jnp.transpose(jnp.broadcast_to(oy, (nobs, nobs))))
    for b in range(batches):
        prior = prior_ref[b]
        average = jnp.mean(prior, axis=0, keepdims=True)
        anomaly = prior - average
        spread = jnp.sum(anomaly * anomaly, axis=0, keepdims=True) / (members - 1) + EPSILON
        noise = errors_ref[b : b + 1, :]
        post_var = 1.0 / (1.0 / spread + 1.0 / noise)
        post_mean = post_var * (average / spread + values_ref[b : b + 1, :] / noise)
        increment = post_mean - average + (jnp.sqrt(post_var / spread) - 1.0) * anomaly
        for later in range(b + 1, batches):
            there = prior_ref[later]
            deviation = there - jnp.mean(there, axis=0, keepdims=True)
            scaled = anomaly * (pair_weight[b, later] / spread / (members - 1))
            covariance = lax.dot_general(
                scaled,
                deviation,
                (((0,), (0,)), ((), ())),
                precision=lax.Precision.HIGHEST,
                preferred_element_type=F32,
            )
            dx = cols_x[b] - rows_x[later]
            dy = cols_y[b] - rows_y[later]
            gain = covariance / (1.0 + (dx * dx + dy * dy))
            prior_ref[later] = there + jnp.dot(
                increment, gain, precision=lax.Precision.HIGHEST, preferred_element_type=F32
            )
        scaled = anomaly * (weight_ref[b : b + 1, :] / spread / (members - 1))
        high, low = split_two(scaled)
        stacked = jnp.concatenate([high, high, low], axis=0).astype(F32)
        wide = a_ref.shape[2]
        if wide > stacked.shape[0]:
            stacked = jnp.concatenate(
                [stacked, jnp.zeros((wide - stacked.shape[0], nobs), F32)], axis=0
            )
        a_ref[b] = jnp.transpose(stacked).astype(BF16)
        high, low = split_two(increment)
        w_ref[b, :members, :nobs] = high
        w_ref[b, :members, nobs:] = high
        w_ref[b, members:, :nobs] = low
        w_ref[b, members:, nobs:] = low
        x_ref[b] = cols_x[b]
        for piece in range(tile_cols // nobs):
            lanes = slice(piece * nobs, (piece + 1) * nobs)
            grid = lax.broadcasted_iota(jnp.int32, (nobs, nobs), 1) + (
                col_at * tile_cols + piece * nobs
            )
            away = cols_y[b] - grid.astype(F32) * inverse
            y_ref[b, :, lanes] = away * away


def update_body(state_ref, a_ref, w_ref, x_ref, y_ref, out_ref, *, first, tile_rows, inverse):
    members, rows, cols = state_ref.shape
    batches, nobs, _ = x_ref.shape
    row_at = lax.axis_index("gx") * tile_rows + first + pl.program_id(0) * rows
    out_ref[...] = state_ref[...]
    for b in range(batches):
        scaled = a_ref[b][:, : 3 * members]
        increment = w_ref[b]
        for r in range(rows):
            state = out_ref[:, r, :]
            deviation = state - jnp.mean(state, axis=0, keepdims=True)
            high, low = split_two(deviation)
            covariance = jnp.dot(
                scaled, jnp.concatenate([high, low, high], axis=0), preferred_element_type=F32
            )
            dx = x_ref[b] - (row_at + r).astype(F32) * inverse
            dx = 1.0 + dx * dx
            away = jnp.concatenate([dx] * (cols // nobs), axis=1) + y_ref[b]
            gain = covariance * pl.reciprocal(away)
            high, low = split_two(gain)
            change = jnp.dot(
                increment, jnp.concatenate([high, low], axis=0), preferred_element_type=F32
            )
            out_ref[:, r, :] = state + (change[:members] + change[members:])


def whole(array):
    return pl.BlockSpec(array.shape, lambda i: (0,) * array.ndim)


def update(state, tables, first, tile_rows, inverse):
    members, here, cols = state.shape
    rows = min(ROWS, here)
    batches, nobs = tables[0].shape[:2]
    cells = here * cols * batches * nobs
    block = pl.BlockSpec((members, rows, cols), lambda i: (0, i, 0))
    return pl.pallas_call(
        functools.partial(update_body, first=first, tile_rows=tile_rows, inverse=inverse),
        grid=(here // rows,),
        in_specs=[block] + [whole(table) for table in tables],
        out_specs=block,
        out_shape=jax.ShapeDtypeStruct(state.shape, F32),
        cost_estimate=pl.CostEstimate(
            flops=cells * members * 10, bytes_accessed=8 * state.size, transcendentals=cells
        ),
        name="update",
    )(state, *tables)


def local(ensemble, obs_values, obs_error, tile_weight, owner_device, obs_cells):
    gx_count = lax.axis_size("gx")
    gy_count = lax.axis_size("gy")
    held, all_rows, tile_cols = ensemble.shape
    members = held * gx_count
    tile_rows = all_rows // gx_count
    batches, nobs = obs_cells.shape
    inverse = 1.0 / (all_rows // 4)
    weight = tile_weight[:, :, 0, 0]
    everyone = gx_count * gy_count
    payload = held * batches + len(pairs_of(batches))
    payload = -(-payload // 8) * 8

    blocks = ensemble.reshape(held, gx_count, tile_rows, tile_cols)
    depth = tile_rows // CHUNKS
    arriving = []
    for c in range(CHUNKS):
        piece = blocks[:, :, c * depth : (c + 1) * depth].transpose(1, 0, 2, 3)
        arriving.append(lax.all_to_all(piece, "gx", split_axis=0, concat_axis=0, tiled=True))

    picked = pl.pallas_call(
        functools.partial(pick_body, tile_rows=tile_rows, gy_count=gy_count),
        in_specs=[
            pl.BlockSpec(memory_space=SMEM),
            pl.BlockSpec(memory_space=VMEM),
            pl.BlockSpec(memory_space=VMEM),
            pl.BlockSpec(memory_space=pl.ANY),
        ],
        out_specs=pl.BlockSpec(memory_space=VMEM),
        out_shape=jax.ShapeDtypeStruct((payload, nobs), F32),
        scratch_shapes=[
            pltpu.VMEM((batches, held, tile_rows, tile_cols), F32),
            pltpu.SemaphoreType.DMA((batches,)),
        ],
        name="pick",
    )(owner_device, obs_cells, weight, ensemble)
    got = lax.all_to_all(
        jnp.broadcast_to(picked[None], (everyone, payload, nobs)),
        ("gx", "gy"),
        split_axis=0,
        concat_axis=0,
        tiled=True,
    )
    wide = -(-3 * members // nobs) * nobs
    tables = pl.pallas_call(
        functools.partial(
            chain_body,
            tile_rows=tile_rows,
            tile_cols=tile_cols,
            held=held,
            gx_count=gx_count,
            gy_count=gy_count,
            inverse=inverse,
        ),
        in_specs=[pl.BlockSpec(memory_space=SMEM)] + [pl.BlockSpec(memory_space=VMEM)] * 5,
        out_specs=[pl.BlockSpec(memory_space=VMEM)] * 4,
        out_shape=[
            jax.ShapeDtypeStruct((batches, nobs, wide), BF16),
            jax.ShapeDtypeStruct((batches, 2 * members, 2 * nobs), BF16),
            jax.ShapeDtypeStruct((batches, nobs, nobs), F32),
            jax.ShapeDtypeStruct((batches, nobs, tile_cols), F32),
        ],
        scratch_shapes=[pltpu.VMEM((batches, members, nobs), F32)],
        name="chain",
    )(owner_device, obs_cells, obs_values, obs_error, weight, got)

    leaving = []
    for c in range(CHUNKS):
        state = arriving[c].reshape(members, depth, tile_cols)
        updated = update(state, tables, c * depth, tile_rows, inverse)
        sent = lax.all_to_all(
            updated.reshape(gx_count, held, depth, tile_cols),
            "gx",
            split_axis=0,
            concat_axis=0,
            tiled=True,
        )
        leaving.append(sent.transpose(1, 0, 2, 3))
    return jnp.concatenate(leaving, axis=2).reshape(ensemble.shape)


def solution(mesh):
    placed = (P("gx", None, "gy"), P(), P(), P(None, None, "gx", "gy"), P(), P())
    return jax.shard_map(
        local, mesh=mesh, in_specs=placed, out_specs=P("gx", None, "gy"), check_vma=False
    )
```

```python
import functools

import jax
import jax.numpy as jnp
from jax import lax
from jax.experimental import pallas as pl
from jax.experimental.pallas import tpu as pltpu
from jax.sharding import PartitionSpec as P


EPSILON = 1e-06
FIRST_EIGHTHS = 4
ROWS = 8
F32 = jnp.float32
BF16 = jnp.bfloat16
VMEM = pltpu.MemorySpace.VMEM
SMEM = pltpu.MemorySpace.SMEM


def split_two(value):
    high = value.astype(BF16)
    low = (value - high.astype(F32)).astype(BF16)
    return high, low


def pairs_of(batches):
    return [(b, later) for b in range(batches) for later in range(b + 1, batches)]


def pick_body(
    owner_ref,
    cells_ref,
    weight_ref,
    ens_ref,
    out_ref,
    blocks_ref,
    window,
    in_sems,
    out_sems,
    *,
    tile_rows,
    gx_count,
    gy_count,
):
    batches, nobs = cells_ref.shape
    held, _, cols = ens_ref.shape
    row_at = lax.axis_index("gx")
    col_at = lax.axis_index("gy")
    me = row_at * gy_count + col_at

    def fetch(tile):
        rows = pl.ds(tile * tile_rows, tile_rows)
        return pltpu.make_async_copy(ens_ref.at[:, rows, :], window.at[tile], in_sems.at[tile])

    def put(tile):
        return pltpu.make_async_copy(window.at[tile], blocks_ref.at[tile], out_sems.at[tile])

    for tile in range(gx_count):
        fetch(tile).start()
    out_ref[...] = jnp.zeros_like(out_ref)
    for at, (b, later) in enumerate(pairs_of(batches)):
        row = held * batches + at
        out_ref[row : row + 1, :] = jnp.where(owner_ref[later] == me, weight_ref[b : b + 1, :], 0.0)
    for tile in range(gx_count):
        fetch(tile).wait()
        put(tile).start()
    for b in range(batches):
        owner_row = owner_ref[b] // gy_count
        cell = cells_ref[b : b + 1, :]
        row_hit = (lax.broadcasted_iota(jnp.int32, (tile_rows, nobs), 0) == cell // cols).astype(F32)
        row_hit = row_hit.astype(BF16)
        row_hit = jnp.concatenate([row_hit] * 3, axis=0)
        col_hit = lax.broadcasted_iota(jnp.int32, (cols, nobs), 0) == cell % cols
        mine = owner_ref[b] % gy_count == col_at
        for m in range(held):
            values = window[owner_row, m]
            high = values.astype(BF16)
            rest = values - high.astype(F32)
            middle, low = split_two(rest)
            stacked = jnp.concatenate([high, middle, low], axis=0)
            columns = lax.dot_general(
                stacked, row_hit, (((0,), (0,)), ((), ())), preferred_element_type=F32
            )
            picked = jnp.sum(jnp.where(col_hit, columns, 0.0), axis=0, keepdims=True)
            row = m * batches + b
            out_ref[row : row + 1, :] = jnp.where(mine, picked, 0.0)
    for tile in range(gx_count):
        put(tile).wait()


def observed_at(owner_ref, cells_ref, b, tile_rows, tile_cols, gy_count, inverse):
    nobs = cells_ref.shape[1]
    cell = cells_ref[b : b + 1, :]
    owner = owner_ref[b]
    ox = ((owner // gy_count) * tile_rows + cell // tile_cols).astype(F32) * inverse
    oy = ((owner % gy_count) * tile_cols + cell % tile_cols).astype(F32) * inverse
    down_x = jnp.transpose(jnp.broadcast_to(ox, (nobs, nobs)))
    down_y = jnp.transpose(jnp.broadcast_to(oy, (nobs, nobs)))
    return ox, oy, down_x, down_y


def tables_body(
    owner_ref, cells_ref, x_ref, y_ref, *, tile_rows, tile_cols, gy_count, inverse
):
    batches, nobs = cells_ref.shape
    left = lax.axis_index("gy") * tile_cols
    for b in range(batches):
        _, _, down_x, down_y = observed_at(
            owner_ref, cells_ref, b, tile_rows, tile_cols, gy_count, inverse
        )
        x_ref[b] = down_x
        for piece in range(tile_cols // nobs):
            lanes = slice(piece * nobs, (piece + 1) * nobs)
            grid = lax.broadcasted_iota(jnp.int32, (nobs, nobs), 1) + (left + piece * nobs)
            away = down_y - grid.astype(F32) * inverse
            y_ref[b, :, lanes] = away * away


def chain_body(
    owner_ref,
    cells_ref,
    values_ref,
    errors_ref,
    weight_ref,
    got_ref,
    a_ref,
    w_ref,
    prior_ref,
    *,
    tile_rows,
    tile_cols,
    held,
    gy_count,
    offsets,
    inverse,
):
    batches, nobs = cells_ref.shape
    members = held * len(offsets)
    weights = jnp.zeros(got_ref.shape[1:], F32)
    row_at = lax.axis_index("gx")
    for slot, offset in enumerate(offsets):
        part = got_ref[slot]
        weights = weights + part
        source = held * (row_at ^ offset)
        for m in range(held):
            for b in range(batches):
                row = m * batches + b
                prior_ref[b, pl.ds(source + m, 1), :] = part[row : row + 1, :]
    pair_weight = {
        pair: weights[held * batches + at : held * batches + at + 1, :]
        for at, pair in enumerate(pairs_of(batches))
    }
    places = [
        observed_at(owner_ref, cells_ref, b, tile_rows, tile_cols, gy_count, inverse)
        for b in range(batches)
    ]
    for b in range(batches):
        prior = prior_ref[b]
        average = jnp.mean(prior, axis=0, keepdims=True)
        anomaly = prior - average
        spread = jnp.sum(anomaly * anomaly, axis=0, keepdims=True) / (members - 1) + EPSILON
        noise = errors_ref[b : b + 1, :]
        post_var = 1.0 / (1.0 / spread + 1.0 / noise)
        post_mean = post_var * (average / spread + values_ref[b : b + 1, :] / noise)
        increment = post_mean - average + (jnp.sqrt(post_var / spread) - 1.0) * anomaly
        for later in range(b + 1, batches):
            there = prior_ref[later]
            deviation = there - jnp.mean(there, axis=0, keepdims=True)
            scaled = anomaly * (pair_weight[b, later] / spread / (members - 1))
            covariance = lax.dot_general(
                scaled,
                deviation,
                (((0,), (0,)), ((), ())),
                precision=lax.Precision.HIGHEST,
                preferred_element_type=F32,
            )
            dx = places[b][2] - places[later][0]
            dy = places[b][3] - places[later][1]
            gain = covariance / (1.0 + (dx * dx + dy * dy))
            prior_ref[later] = there + jnp.dot(
                increment, gain, precision=lax.Precision.HIGHEST, preferred_element_type=F32
            )
        scaled = anomaly * (weight_ref[b : b + 1, :] / spread / (members - 1))
        high, low = split_two(scaled)
        stacked = jnp.concatenate([high, high, low], axis=0).astype(F32)
        wide = a_ref.shape[2]
        if wide > stacked.shape[0]:
            stacked = jnp.concatenate(
                [stacked, jnp.zeros((wide - stacked.shape[0], nobs), F32)], axis=0
            )
        a_ref[b] = jnp.transpose(stacked).astype(BF16)
        high, low = split_two(increment)
        w_ref[b, :members, :nobs] = high
        w_ref[b, :members, nobs:] = high
        w_ref[b, members:, :nobs] = low
        w_ref[b, members:, nobs:] = low


def update_body(
    state_ref, a_ref, w_ref, x_ref, y_ref, *refs, first, tile_rows, held, inverse, spread_out
):
    members, rows, cols = state_ref.shape
    batches, nobs, _ = x_ref.shape
    row_at = lax.axis_index("gx")
    top = row_at * tile_rows + first + pl.program_id(0) * rows
    states = [state_ref[:, r, :] for r in range(rows)]
    for b in range(batches):
        scaled = a_ref[b][:, : 3 * members]
        increment = w_ref[b]
        for r in range(rows):
            state = states[r]
            deviation = state - jnp.mean(state, axis=0, keepdims=True)
            high, low = split_two(deviation)
            covariance = jnp.dot(
                scaled, jnp.concatenate([high, low, high], axis=0), preferred_element_type=F32
            )
            dx = x_ref[b] - (top + r).astype(F32) * inverse
            dx = 1.0 + dx * dx
            away = jnp.concatenate([dx] * (cols // nobs), axis=1) + y_ref[b]
            gain = covariance * pl.reciprocal(away)
            high, low = split_two(gain)
            change = jnp.dot(
                increment, jnp.concatenate([high, low], axis=0), preferred_element_type=F32
            )
            states[r] = state + (change[:members] + change[members:])
    if spread_out:
        outs, whole_ref = refs[:-1], refs[-1]
    else:
        outs, whole_ref = (), refs[0]
    for r in range(rows):
        whole_ref[:, r, :] = states[r]
    for slot, out_ref in enumerate(outs):
        out_ref[...] = whole_ref[pl.ds(held * (row_at ^ slot), held)]


def share(picked, gx_count, gy_count):
    got = picked[None]
    offsets = [0]

    def gather(got, step):
        other = lax.ppermute(got, "gx", [(i, i ^ step) for i in range(gx_count)])
        return jnp.concatenate([got, other], axis=0)

    steps = [1 << bit for bit in range(gx_count.bit_length() - 1)]
    far = steps[-1:]
    for step in far:
        got = gather(got, step)
        offsets = offsets + [offset ^ step for offset in offsets]
    others = [
        lax.ppermute(got, "gy", [(i, i ^ step) for i in range(gy_count)])
        for step in range(1, gy_count)
    ]
    for other in others:
        got = got + other
    for step in steps[:-1]:
        got = gather(got, step)
        offsets = offsets + [offset ^ step for offset in offsets]
    return got, offsets


def whole(array):
    return pl.BlockSpec(array.shape, lambda i: (0,) * array.ndim)


def update(state, tables, first, depth, tile_rows, inverse, gx_count, spread_out):
    members, _, cols = state.shape
    rows = ROWS
    held = members // gx_count
    batches, nobs = tables[0].shape[:2]
    cells = depth * cols * batches * nobs
    start = first // rows
    if spread_out:
        out_specs = [pl.BlockSpec((held, rows, cols), lambda i: (0, i, 0))] * gx_count
        out_shape = [jax.ShapeDtypeStruct((held, depth, cols), F32)] * gx_count
        scratch = [pltpu.VMEM((members, rows, cols), F32)]
    else:
        out_specs = pl.BlockSpec((members, rows, cols), lambda i: (0, i, 0))
        out_shape = jax.ShapeDtypeStruct((members, depth, cols), F32)
        scratch = []
    return pl.pallas_call(
        functools.partial(
            update_body,
            first=first,
            tile_rows=tile_rows,
            inverse=inverse,
            held=held,
            spread_out=spread_out,
        ),
        grid=(depth // rows,),
        in_specs=[
            pl.BlockSpec((members, rows, cols), lambda i: (0, start + i, 0)),
            whole(tables[0]),
            whole(tables[1]),
            whole(tables[2]),
            whole(tables[3]),
        ],
        out_specs=out_specs,
        out_shape=out_shape,
        scratch_shapes=scratch,
        cost_estimate=pl.CostEstimate(
            flops=cells * members * 10,
            bytes_accessed=8 * members * depth * cols,
            transcendentals=cells,
        ),
        name="update",
    )(state, *tables)


def assemble_body(whole_ref, *refs, first, tile_rows, here):
    pieces, out_ref, sems = refs[:-2], refs[-2], refs[-1]
    row_at = lax.axis_index("gx")
    copies = []
    for tile in range(whole_ref.shape[0]):
        rows = pl.ds(tile * tile_rows, first)
        copies.append(
            pltpu.make_async_copy(whole_ref.at[tile], out_ref.at[:, rows, :], sems.at[tile])
        )
    for slot, piece in enumerate(pieces):
        start = pl.multiple_of((row_at ^ slot) * tile_rows + first, here)
        rows = pl.ds(start, tile_rows - first)
        copies.append(
            pltpu.make_async_copy(
                piece, out_ref.at[:, rows, :], sems.at[whole_ref.shape[0] + slot]
            )
        )
    for copy in copies:
        copy.start()
    for copy in copies:
        copy.wait()


def local(ensemble, obs_values, obs_error, tile_weight, owner_device, obs_cells):
    gx_count = lax.axis_size("gx")
    gy_count = lax.axis_size("gy")
    held, all_rows, tile_cols = ensemble.shape
    members = held * gx_count
    tile_rows = all_rows // gx_count
    batches, nobs = obs_cells.shape
    inverse = 1.0 / (all_rows // 4)
    weight = tile_weight[:, :, 0, 0]
    payload = held * batches + len(pairs_of(batches))
    payload = -(-payload // 8) * 8
    in_smem = pl.BlockSpec(memory_space=SMEM)
    in_vmem = pl.BlockSpec(memory_space=VMEM)
    anywhere = pl.BlockSpec(memory_space=pl.ANY)
    geometry = dict(tile_rows=tile_rows, tile_cols=tile_cols, gy_count=gy_count, inverse=inverse)

    picked, blocks = pl.pallas_call(
        functools.partial(pick_body, tile_rows=tile_rows, gx_count=gx_count, gy_count=gy_count),
        in_specs=[in_smem, in_vmem, in_vmem, anywhere],
        out_specs=[in_vmem, anywhere],
        out_shape=[
            jax.ShapeDtypeStruct((payload, nobs), F32),
            jax.ShapeDtypeStruct((gx_count, held, tile_rows, tile_cols), F32),
        ],
        scratch_shapes=[
            pltpu.VMEM((gx_count, held, tile_rows, tile_cols), F32),
            pltpu.SemaphoreType.DMA((gx_count,)),
            pltpu.SemaphoreType.DMA((gx_count,)),
        ],
        name="pick",
    )(owner_device, obs_cells, weight, ensemble)
    state = lax.all_to_all(blocks, "gx", split_axis=0, concat_axis=0, tiled=True)
    state = state.reshape(members, tile_rows, tile_cols)
    places = pl.pallas_call(
        functools.partial(tables_body, **geometry),
        in_specs=[in_smem, in_vmem],
        out_specs=[in_vmem] * 2,
        out_shape=[
            jax.ShapeDtypeStruct((batches, nobs, nobs), F32),
            jax.ShapeDtypeStruct((batches, nobs, tile_cols), F32),
        ],
        name="tables",
    )(owner_device, obs_cells)
    got, offsets = share(picked, gx_count, gy_count)
    wide = -(-3 * members // nobs) * nobs
    factors = pl.pallas_call(
        functools.partial(chain_body, held=held, offsets=offsets, **geometry),
        in_specs=[in_smem] + [in_vmem] * 5,
        out_specs=[in_vmem] * 2,
        out_shape=[
            jax.ShapeDtypeStruct((batches, nobs, wide), BF16),
            jax.ShapeDtypeStruct((batches, 2 * members, 2 * nobs), BF16),
        ],
        scratch_shapes=[pltpu.VMEM((batches, members, nobs), F32)],
        name="chain",
    )(owner_device, obs_cells, obs_values, obs_error, weight, got)
    tables = [*factors, *places]

    first = tile_rows * FIRST_EIGHTHS // 8
    rest = tile_rows - first
    upper = update(state, tables, 0, first, tile_rows, inverse, gx_count, False)
    upper = lax.all_to_all(
        upper.reshape(gx_count, held, first, tile_cols),
        "gx",
        split_axis=0,
        concat_axis=0,
        tiled=True,
    )
    lower = update(state, tables, first, rest, tile_rows, inverse, gx_count, True)
    lower = [
        piece
        if slot == 0
        else lax.ppermute(piece, "gx", [(i, i ^ slot) for i in range(gx_count)])
        for slot, piece in enumerate(lower)
    ]
    return pl.pallas_call(
        functools.partial(assemble_body, first=first, tile_rows=tile_rows, here=ROWS),
        in_specs=[in_vmem] * (1 + gx_count),
        out_specs=anywhere,
        out_shape=jax.ShapeDtypeStruct(ensemble.shape, F32),
        scratch_shapes=[pltpu.SemaphoreType.DMA((2 * gx_count,))],
        name="assemble",
    )(upper, *lower)


def solution(mesh):
    placed = (P("gx", None, "gy"), P(), P(), P(None, None, "gx", "gy"), P(), P())
    return jax.shard_map(
        local, mesh=mesh, in_specs=placed, out_specs=P("gx", None, "gy"), check_vma=False
    )
```

```python
import functools

import jax
import jax.numpy as jnp
from jax import lax
from jax.experimental import pallas as pl
from jax.experimental.pallas import tpu as pltpu
from jax.sharding import PartitionSpec as P


EPSILON = 1e-06
FIRST_EIGHTHS = 3
LIGHT = pltpu.CompilerParams(vmem_limit_bytes=16 << 20)
ROWS = 8
F32 = jnp.float32
BF16 = jnp.bfloat16
VMEM = pltpu.MemorySpace.VMEM
SMEM = pltpu.MemorySpace.SMEM


def split_two(value):
    high = value.astype(BF16)
    low = (value - high.astype(F32)).astype(BF16)
    return high, low


def pairs_of(batches):
    return [(b, later) for b in range(batches) for later in range(b + 1, batches)]


def pick_body(
    owner_ref,
    cells_ref,
    weight_ref,
    ens_ref,
    out_ref,
    blocks_ref,
    window,
    in_sems,
    out_sems,
    *,
    tile_rows,
    gx_count,
    gy_count,
):
    batches, nobs = cells_ref.shape
    held, _, cols = ens_ref.shape
    row_at = lax.axis_index("gx")
    col_at = lax.axis_index("gy")
    me = row_at * gy_count + col_at

    def fetch(tile):
        rows = pl.ds(tile * tile_rows, tile_rows)
        return pltpu.make_async_copy(ens_ref.at[:, rows, :], window.at[tile], in_sems.at[tile])

    def put(tile):
        return pltpu.make_async_copy(window.at[tile], blocks_ref.at[tile], out_sems.at[tile])

    for tile in range(gx_count):
        fetch(tile).start()
    out_ref[...] = jnp.zeros_like(out_ref)
    for at, (b, later) in enumerate(pairs_of(batches)):
        row = held * batches + at
        out_ref[row : row + 1, :] = jnp.where(owner_ref[later] == me, weight_ref[b : b + 1, :], 0.0)
    for tile in range(gx_count):
        fetch(tile).wait()
        put(tile).start()
    for b in range(batches):
        owner_row = owner_ref[b] // gy_count
        cell = cells_ref[b : b + 1, :]
        row_hit = (lax.broadcasted_iota(jnp.int32, (tile_rows, nobs), 0) == cell // cols).astype(F32)
        row_hit = row_hit.astype(BF16)
        row_hit = jnp.concatenate([row_hit] * 3, axis=0)
        col_hit = lax.broadcasted_iota(jnp.int32, (cols, nobs), 0) == cell % cols
        mine = owner_ref[b] % gy_count == col_at
        for m in range(held):
            values = window[owner_row, m]
            high = values.astype(BF16)
            rest = values - high.astype(F32)
            middle, low = split_two(rest)
            stacked = jnp.concatenate([high, middle, low], axis=0)
            columns = lax.dot_general(
                stacked, row_hit, (((0,), (0,)), ((), ())), preferred_element_type=F32
            )
            picked = jnp.sum(jnp.where(col_hit, columns, 0.0), axis=0, keepdims=True)
            row = m * batches + b
            out_ref[row : row + 1, :] = jnp.where(mine, picked, 0.0)
    for tile in range(gx_count):
        put(tile).wait()


def observed_at(owner_ref, cells_ref, b, tile_rows, tile_cols, gy_count, inverse):
    nobs = cells_ref.shape[1]
    cell = cells_ref[b : b + 1, :]
    owner = owner_ref[b]
    ox = ((owner // gy_count) * tile_rows + cell // tile_cols).astype(F32) * inverse
    oy = ((owner % gy_count) * tile_cols + cell % tile_cols).astype(F32) * inverse
    down_x = jnp.transpose(jnp.broadcast_to(ox, (nobs, nobs)))
    down_y = jnp.transpose(jnp.broadcast_to(oy, (nobs, nobs)))
    return ox, oy, down_x, down_y


def tables_body(
    owner_ref, cells_ref, x_ref, y_ref, *, tile_rows, tile_cols, gy_count, inverse
):
    batches, nobs = cells_ref.shape
    left = lax.axis_index("gy") * tile_cols
    for b in range(batches):
        _, _, down_x, down_y = observed_at(
            owner_ref, cells_ref, b, tile_rows, tile_cols, gy_count, inverse
        )
        x_ref[b] = down_x
        for piece in range(tile_cols // nobs):
            lanes = slice(piece * nobs, (piece + 1) * nobs)
            grid = lax.broadcasted_iota(jnp.int32, (nobs, nobs), 1) + (left + piece * nobs)
            away = down_y - grid.astype(F32) * inverse
            y_ref[b, :, lanes] = away * away


def chain_body(
    owner_ref,
    cells_ref,
    values_ref,
    errors_ref,
    weight_ref,
    got_ref,
    a_ref,
    w_ref,
    prior_ref,
    *,
    tile_rows,
    tile_cols,
    held,
    gy_count,
    offsets,
    inverse,
):
    batches, nobs = cells_ref.shape
    members = held * len(offsets)
    weights = jnp.zeros(got_ref.shape[1:], F32)
    row_at = lax.axis_index("gx")
    for slot, offset in enumerate(offsets):
        part = got_ref[slot]
        weights = weights + part
        source = held * (row_at ^ offset)
        for m in range(held):
            for b in range(batches):
                row = m * batches + b
                prior_ref[b, pl.ds(source + m, 1), :] = part[row : row + 1, :]
    pair_weight = {
        pair: weights[held * batches + at : held * batches + at + 1, :]
        for at, pair in enumerate(pairs_of(batches))
    }
    places = [
        observed_at(owner_ref, cells_ref, b, tile_rows, tile_cols, gy_count, inverse)
        for b in range(batches)
    ]
    for b in range(batches):
        prior = prior_ref[b]
        average = jnp.mean(prior, axis=0, keepdims=True)
        anomaly = prior - average
        spread = jnp.sum(anomaly * anomaly, axis=0, keepdims=True) / (members - 1) + EPSILON
        noise = errors_ref[b : b + 1, :]
        post_var = 1.0 / (1.0 / spread + 1.0 / noise)
        post_mean = post_var * (average / spread + values_ref[b : b + 1, :] / noise)
        increment = post_mean - average + (jnp.sqrt(post_var / spread) - 1.0) * anomaly
        for later in range(b + 1, batches):
            there = prior_ref[later]
            deviation = there - jnp.mean(there, axis=0, keepdims=True)
            scaled = anomaly * (pair_weight[b, later] / spread / (members - 1))
            covariance = lax.dot_general(
                scaled,
                deviation,
                (((0,), (0,)), ((), ())),
                precision=lax.Precision.HIGHEST,
                preferred_element_type=F32,
            )
            dx = places[b][2] - places[later][0]
            dy = places[b][3] - places[later][1]
            gain = covariance / (1.0 + (dx * dx + dy * dy))
            prior_ref[later] = there + jnp.dot(
                increment, gain, precision=lax.Precision.HIGHEST, preferred_element_type=F32
            )
        scaled = anomaly * (weight_ref[b : b + 1, :] / spread / (members - 1))
        high, low = split_two(scaled)
        stacked = jnp.concatenate([high, high, low], axis=0).astype(F32)
        wide = a_ref.shape[2]
        if wide > stacked.shape[0]:
            stacked = jnp.concatenate(
                [stacked, jnp.zeros((wide - stacked.shape[0], nobs), F32)], axis=0
            )
        a_ref[b] = jnp.transpose(stacked).astype(BF16)
        high, low = split_two(increment)
        w_ref[b, :members, :nobs] = high
        w_ref[b, :members, nobs:] = high
        w_ref[b, members:, :nobs] = low
        w_ref[b, members:, nobs:] = low


def update_body(
    state_ref, a_ref, w_ref, x_ref, y_ref, *refs, first, tile_rows, held, inverse, spread_out
):
    members, rows, cols = state_ref.shape
    batches, nobs, _ = x_ref.shape
    row_at = lax.axis_index("gx")
    top = row_at * tile_rows + first + pl.program_id(0) * rows
    states = [state_ref[:, r, :] for r in range(rows)]
    for b in range(batches):
        scaled = a_ref[b][:, : 3 * members]
        increment = w_ref[b]
        for r in range(rows):
            state = states[r]
            deviation = state - jnp.mean(state, axis=0, keepdims=True)
            high, low = split_two(deviation)
            covariance = jnp.dot(
                scaled, jnp.concatenate([high, low, high], axis=0), preferred_element_type=F32
            )
            dx = x_ref[b] - (top + r).astype(F32) * inverse
            dx = 1.0 + dx * dx
            away = jnp.concatenate([dx] * (cols // nobs), axis=1) + y_ref[b]
            gain = covariance * pl.reciprocal(away)
            high, low = split_two(gain)
            change = jnp.dot(
                increment, jnp.concatenate([high, low], axis=0), preferred_element_type=F32
            )
            states[r] = state + (change[:members] + change[members:])
    if spread_out:
        outs, whole_ref = refs[:-1], refs[-1]
    else:
        outs, whole_ref = (), refs[0]
    for r in range(rows):
        whole_ref[:, r, :] = states[r]
    for slot, out_ref in enumerate(outs):
        out_ref[...] = whole_ref[pl.ds(held * (row_at ^ slot), held)]


def share(picked, gx_count, gy_count):
    got = picked[None]
    offsets = [0]

    def gather(got, step):
        other = lax.ppermute(got, "gx", [(i, i ^ step) for i in range(gx_count)])
        return jnp.concatenate([got, other], axis=0)

    steps = [1 << bit for bit in range(gx_count.bit_length() - 1)]
    far = steps[-1:]
    for step in far:
        got = gather(got, step)
        offsets = offsets + [offset ^ step for offset in offsets]
    others = [
        lax.ppermute(got, "gy", [(i, i ^ step) for i in range(gy_count)])
        for step in range(1, gy_count)
    ]
    for other in others:
        got = got + other
    for step in steps[:-1]:
        got = gather(got, step)
        offsets = offsets + [offset ^ step for offset in offsets]
    return got, offsets


def whole(array):
    return pl.BlockSpec(array.shape, lambda i: (0,) * array.ndim)


def update(state, tables, first, depth, tile_rows, inverse, gx_count, spread_out):
    members, _, cols = state.shape
    rows = ROWS
    held = members // gx_count
    batches, nobs = tables[0].shape[:2]
    cells = depth * cols * batches * nobs
    start = first // rows
    if spread_out:
        out_specs = [pl.BlockSpec((held, rows, cols), lambda i: (0, i, 0))] * gx_count
        out_shape = [jax.ShapeDtypeStruct((held, depth, cols), F32)] * gx_count
        scratch = [pltpu.VMEM((members, rows, cols), F32)]
    else:
        out_specs = pl.BlockSpec((members, rows, cols), lambda i: (0, i, 0))
        out_shape = jax.ShapeDtypeStruct((members, depth, cols), F32)
        scratch = []
    return pl.pallas_call(
        functools.partial(
            update_body,
            first=first,
            tile_rows=tile_rows,
            inverse=inverse,
            held=held,
            spread_out=spread_out,
        ),
        grid=(depth // rows,),
        in_specs=[
            pl.BlockSpec((members, rows, cols), lambda i: (0, start + i, 0)),
            whole(tables[0]),
            whole(tables[1]),
            whole(tables[2]),
            whole(tables[3]),
        ],
        out_specs=out_specs,
        out_shape=out_shape,
        scratch_shapes=scratch,
        cost_estimate=pl.CostEstimate(
            flops=cells * members * 10,
            bytes_accessed=8 * members * depth * cols,
            transcendentals=cells,
        ),
        compiler_params=LIGHT,
        name="update",
    )(state, *tables)


def assemble_body(whole_ref, *refs, first, tile_rows, here):
    pieces, out_ref, sems = refs[:-2], refs[-2], refs[-1]
    row_at = lax.axis_index("gx")
    copies = []
    for tile in range(whole_ref.shape[0]):
        rows = pl.ds(tile * tile_rows, first)
        copies.append(
            pltpu.make_async_copy(whole_ref.at[tile], out_ref.at[:, rows, :], sems.at[tile])
        )
    for slot, piece in enumerate(pieces):
        start = pl.multiple_of((row_at ^ slot) * tile_rows + first, here)
        rows = pl.ds(start, tile_rows - first)
        copies.append(
            pltpu.make_async_copy(
                piece, out_ref.at[:, rows, :], sems.at[whole_ref.shape[0] + slot]
            )
        )
    for copy in copies:
        copy.start()
    for copy in copies:
        copy.wait()


def local(ensemble, obs_values, obs_error, tile_weight, owner_device, obs_cells):
    gx_count = lax.axis_size("gx")
    gy_count = lax.axis_size("gy")
    held, all_rows, tile_cols = ensemble.shape
    members = held * gx_count
    tile_rows = all_rows // gx_count
    batches, nobs = obs_cells.shape
    inverse = 1.0 / (all_rows // 4)
    weight = tile_weight[:, :, 0, 0]
    payload = held * batches + len(pairs_of(batches))
    payload = -(-payload // 8) * 8
    in_smem = pl.BlockSpec(memory_space=SMEM)
    in_vmem = pl.BlockSpec(memory_space=VMEM)
    anywhere = pl.BlockSpec(memory_space=pl.ANY)
    geometry = dict(tile_rows=tile_rows, tile_cols=tile_cols, gy_count=gy_count, inverse=inverse)

    picked, blocks = pl.pallas_call(
        functools.partial(pick_body, tile_rows=tile_rows, gx_count=gx_count, gy_count=gy_count),
        in_specs=[in_smem, in_vmem, in_vmem, anywhere],
        out_specs=[in_vmem, anywhere],
        out_shape=[
            jax.ShapeDtypeStruct((payload, nobs), F32),
            jax.ShapeDtypeStruct((gx_count, held, tile_rows, tile_cols), F32),
        ],
        scratch_shapes=[
            pltpu.VMEM((gx_count, held, tile_rows, tile_cols), F32),
            pltpu.SemaphoreType.DMA((gx_count,)),
            pltpu.SemaphoreType.DMA((gx_count,)),
        ],
        name="pick",
    )(owner_device, obs_cells, weight, ensemble)
    state = lax.all_to_all(blocks, "gx", split_axis=0, concat_axis=0, tiled=True)
    state = state.reshape(members, tile_rows, tile_cols)
    places = pl.pallas_call(
        functools.partial(tables_body, **geometry),
        in_specs=[in_smem, in_vmem],
        out_specs=[in_vmem] * 2,
        out_shape=[
            jax.ShapeDtypeStruct((batches, nobs, nobs), F32),
            jax.ShapeDtypeStruct((batches, nobs, tile_cols), F32),
        ],
        compiler_params=LIGHT,
        name="tables",
    )(owner_device, obs_cells)
    got, offsets = share(picked, gx_count, gy_count)
    wide = -(-3 * members // nobs) * nobs
    factors = pl.pallas_call(
        functools.partial(chain_body, held=held, offsets=offsets, **geometry),
        in_specs=[in_smem] + [in_vmem] * 5,
        out_specs=[in_vmem] * 2,
        out_shape=[
            jax.ShapeDtypeStruct((batches, nobs, wide), BF16),
            jax.ShapeDtypeStruct((batches, 2 * members, 2 * nobs), BF16),
        ],
        scratch_shapes=[pltpu.VMEM((batches, members, nobs), F32)],
        compiler_params=LIGHT,
        name="chain",
    )(owner_device, obs_cells, obs_values, obs_error, weight, got)
    tables = [*factors, *places]

    first = tile_rows * FIRST_EIGHTHS // 8
    rest = tile_rows - first
    upper = update(state, tables, 0, first, tile_rows, inverse, gx_count, False)
    upper = lax.all_to_all(
        upper.reshape(gx_count, held, first, tile_cols),
        "gx",
        split_axis=0,
        concat_axis=0,
        tiled=True,
    )
    lower = [*update(state, tables, first, rest, tile_rows, inverse, gx_count, True)]
    for slot in range(1, gx_count):
        lower[slot] = lax.ppermute(
            lower[slot], "gx", [(i, i ^ slot) for i in range(gx_count)]
        )
    return pl.pallas_call(
        functools.partial(assemble_body, first=first, tile_rows=tile_rows, here=ROWS),
        in_specs=[in_vmem] * (1 + gx_count),
        out_specs=anywhere,
        out_shape=jax.ShapeDtypeStruct(ensemble.shape, F32),
        scratch_shapes=[pltpu.SemaphoreType.DMA((2 * gx_count,))],
        compiler_params=LIGHT,
        name="assemble",
    )(upper, *lower)


def solution(mesh):
    placed = (P("gx", None, "gy"), P(), P(), P(None, None, "gx", "gy"), P(), P())
    return jax.shard_map(
        local, mesh=mesh, in_specs=placed, out_specs=P("gx", None, "gy"), check_vma=False
    )
```

```python
import functools

import jax
import jax.numpy as jnp
from jax import lax
from jax.experimental import pallas as pl
from jax.experimental.pallas import tpu as pltpu
from jax.sharding import PartitionSpec as P


EPSILON = 1e-06
FIRST_EIGHTHS = 3
LIGHT = pltpu.CompilerParams(vmem_limit_bytes=16 << 20)
ROWS = 8
F32 = jnp.float32
BF16 = jnp.bfloat16
VMEM = pltpu.MemorySpace.VMEM
SMEM = pltpu.MemorySpace.SMEM


def split_two(value):
    high = value.astype(BF16)
    low = (value - high.astype(F32)).astype(BF16)
    return high, low


def pairs_of(batches):
    return [(b, later) for b in range(batches) for later in range(b + 1, batches)]


def pick_body(
    owner_in,
    cells_in,
    weight_in,
    ens_ref,
    out_ref,
    blocks_ref,
    *refs,
    tile_rows,
    first,
    gx_count,
    gy_count,
):
    pieces = refs[:gx_count]
    window, owner_ref, cells_ref, weight_ref, in_sems, out_sems, small_sems = refs[gx_count:]
    batches, nobs = cells_ref.shape
    held, _, cols = ens_ref.shape
    row_at = lax.axis_index("gx")
    col_at = lax.axis_index("gy")
    me = row_at * gy_count + col_at

    def fetch(tile):
        rows = pl.ds(tile * tile_rows, tile_rows)
        return pltpu.make_async_copy(ens_ref.at[:, rows, :], window.at[tile], in_sems.at[tile])

    def puts(slot):
        upper = window.at[slot, :, pl.ds(0, first), :]
        lower = window.at[row_at ^ slot, :, pl.ds(first, tile_rows - first), :]
        return (
            pltpu.make_async_copy(upper, blocks_ref.at[slot], out_sems.at[slot]),
            pltpu.make_async_copy(lower, pieces[slot], out_sems.at[gx_count + slot]),
        )

    small = [
        pltpu.make_async_copy(source, target, small_sems.at[at])
        for at, (source, target) in enumerate(
            [(owner_in, owner_ref), (cells_in, cells_ref), (weight_in, weight_ref)]
        )
    ]
    for copy in small:
        copy.start()
    for tile in range(gx_count):
        fetch(tile).start()
    out_ref[...] = jnp.zeros_like(out_ref)
    for copy in small:
        copy.wait()
    for at, (b, later) in enumerate(pairs_of(batches)):
        row = held * batches + at
        out_ref[row : row + 1, :] = jnp.where(owner_ref[later] == me, weight_ref[b : b + 1, :], 0.0)
    hits = []
    for b in range(batches):
        cell = cells_ref[b : b + 1, :]
        row_hit = (lax.broadcasted_iota(jnp.int32, (tile_rows, nobs), 0) == cell // cols).astype(F32)
        row_hit = row_hit.astype(BF16)
        col_hit = lax.broadcasted_iota(jnp.int32, (cols, nobs), 0) == cell % cols
        hits.append((jnp.concatenate([row_hit] * 3, axis=0), col_hit))
    for tile in range(gx_count):
        fetch(tile).wait()
    for slot in range(gx_count):
        for copy in puts(slot):
            copy.start()
    for b in range(batches):
        row_hit, col_hit = hits[b]
        owner_row = owner_ref[b] // gy_count
        mine = owner_ref[b] % gy_count == col_at
        for m in range(held):
            values = window[owner_row, m]
            high = values.astype(BF16)
            rest = values - high.astype(F32)
            middle, low = split_two(rest)
            stacked = jnp.concatenate([high, middle, low], axis=0)
            columns = lax.dot_general(
                stacked, row_hit, (((0,), (0,)), ((), ())), preferred_element_type=F32
            )
            picked = jnp.sum(jnp.where(col_hit, columns, 0.0), axis=0, keepdims=True)
            row = m * batches + b
            out_ref[row : row + 1, :] = jnp.where(mine, picked, 0.0)
    for slot in range(gx_count):
        for copy in puts(slot):
            copy.wait()


def observed_at(owner_ref, cells_ref, b, tile_rows, tile_cols, gy_count, inverse):
    nobs = cells_ref.shape[1]
    cell = cells_ref[b : b + 1, :]
    owner = owner_ref[b]
    ox = ((owner // gy_count) * tile_rows + cell // tile_cols).astype(F32) * inverse
    oy = ((owner % gy_count) * tile_cols + cell % tile_cols).astype(F32) * inverse
    down_x = jnp.transpose(jnp.broadcast_to(ox, (nobs, nobs)))
    down_y = jnp.transpose(jnp.broadcast_to(oy, (nobs, nobs)))
    return ox, oy, down_x, down_y


def tables_body(
    owner_ref, cells_ref, x_ref, y_ref, *, tile_rows, tile_cols, gy_count, inverse
):
    batches, nobs = cells_ref.shape
    left = lax.axis_index("gy") * tile_cols
    for b in range(batches):
        _, _, down_x, down_y = observed_at(
            owner_ref, cells_ref, b, tile_rows, tile_cols, gy_count, inverse
        )
        x_ref[b] = down_x
        for piece in range(tile_cols // nobs):
            lanes = slice(piece * nobs, (piece + 1) * nobs)
            grid = lax.broadcasted_iota(jnp.int32, (nobs, nobs), 1) + (left + piece * nobs)
            away = down_y - grid.astype(F32) * inverse
            y_ref[b, :, lanes] = away * away


def chain_body(
    owner_ref,
    cells_ref,
    values_ref,
    errors_ref,
    weight_ref,
    got_ref,
    other_ref,
    a_ref,
    w_ref,
    prior_ref,
    *,
    tile_rows,
    tile_cols,
    held,
    gy_count,
    offsets,
    inverse,
):
    batches, nobs = cells_ref.shape
    members = held * len(offsets)
    weights = jnp.zeros(got_ref.shape[1:], F32)
    row_at = lax.axis_index("gx")
    half = got_ref.shape[0]
    for slot, offset in enumerate(offsets):
        part = got_ref[slot] if slot < half else other_ref[slot - half]
        weights = weights + part
        source = held * (row_at ^ offset)
        for m in range(held):
            for b in range(batches):
                row = m * batches + b
                prior_ref[b, pl.ds(source + m, 1), :] = part[row : row + 1, :]
    pair_weight = {
        pair: weights[held * batches + at : held * batches + at + 1, :]
        for at, pair in enumerate(pairs_of(batches))
    }
    places = [
        observed_at(owner_ref, cells_ref, b, tile_rows, tile_cols, gy_count, inverse)
        for b in range(batches)
    ]
    for b in range(batches):
        prior = prior_ref[b]
        average = jnp.mean(prior, axis=0, keepdims=True)
        anomaly = prior - average
        spread = jnp.sum(anomaly * anomaly, axis=0, keepdims=True) / (members - 1) + EPSILON
        noise = errors_ref[b : b + 1, :]
        post_var = 1.0 / (1.0 / spread + 1.0 / noise)
        post_mean = post_var * (average / spread + values_ref[b : b + 1, :] / noise)
        increment = post_mean - average + (jnp.sqrt(post_var / spread) - 1.0) * anomaly
        for later in range(b + 1, batches):
            there = prior_ref[later]
            deviation = there - jnp.mean(there, axis=0, keepdims=True)
            scaled = anomaly * (pair_weight[b, later] / spread / (members - 1))
            covariance = lax.dot_general(
                scaled,
                deviation,
                (((0,), (0,)), ((), ())),
                precision=lax.Precision.HIGHEST,
                preferred_element_type=F32,
            )
            dx = places[b][2] - places[later][0]
            dy = places[b][3] - places[later][1]
            gain = covariance / (1.0 + (dx * dx + dy * dy))
            prior_ref[later] = there + jnp.dot(
                increment, gain, precision=lax.Precision.HIGHEST, preferred_element_type=F32
            )
        scaled = anomaly * (weight_ref[b : b + 1, :] / spread / (members - 1))
        high, low = split_two(scaled)
        stacked = jnp.concatenate([high, high, low], axis=0).astype(F32)
        wide = a_ref.shape[2]
        if wide > stacked.shape[0]:
            stacked = jnp.concatenate(
                [stacked, jnp.zeros((wide - stacked.shape[0], nobs), F32)], axis=0
            )
        a_ref[b] = jnp.transpose(stacked).astype(BF16)
        high, low = split_two(increment)
        w_ref[b, :members, :nobs] = high
        w_ref[b, :members, nobs:] = high
        w_ref[b, members:, :nobs] = low
        w_ref[b, members:, nobs:] = low


def update_body(a_ref, w_ref, x_ref, y_ref, *refs, first, tile_rows, parts, inverse):
    sources, targets = refs[:parts], refs[parts : 2 * parts]
    held, rows, cols = sources[0].shape
    members = held * parts
    batches, nobs, _ = x_ref.shape
    row_at = lax.axis_index("gx")
    top = row_at * tile_rows + first + pl.program_id(0) * rows
    if parts == 1:
        from_ref, to_ref = sources[0], targets[0]
    else:
        from_ref = to_ref = refs[-1]
        for slot, source in enumerate(sources):
            from_ref[pl.ds(held * (row_at ^ slot), held)] = source[...]
    states = [from_ref[:, r, :] for r in range(rows)]
    for b in range(batches):
        scaled = a_ref[b][:, : 3 * members]
        increment = w_ref[b]
        for r in range(rows):
            state = states[r]
            deviation = state - jnp.mean(state, axis=0, keepdims=True)
            high, low = split_two(deviation)
            covariance = jnp.dot(
                scaled, jnp.concatenate([high, low, high], axis=0), preferred_element_type=F32
            )
            dx = x_ref[b] - (top + r).astype(F32) * inverse
            dx = 1.0 + dx * dx
            away = jnp.concatenate([dx] * (cols // nobs), axis=1) + y_ref[b]
            gain = covariance * pl.reciprocal(away)
            high, low = split_two(gain)
            change = jnp.dot(
                increment, jnp.concatenate([high, low], axis=0), preferred_element_type=F32
            )
            states[r] = state + (change[:members] + change[members:])
    for r in range(rows):
        to_ref[:, r, :] = states[r]
    if parts > 1:
        for slot, target in enumerate(targets):
            target[...] = to_ref[pl.ds(held * (row_at ^ slot), held)]


def share(picked, gx_count, gy_count):
    def swap(array, axis, count, step):
        return lax.ppermute(array, axis, [(i, i ^ step) for i in range(count)])

    got = [picked[None]]
    offsets = [0]
    for step in range(2, gx_count, 2):
        got.append(swap(picked[None], "gx", gx_count, step))
        offsets.append(step)
    got = jnp.concatenate(got, axis=0)
    others = []
    for step in range(1, gy_count):
        others.append(swap(got, "gy", gy_count, step))
    for other in others:
        got = got + other
    other = swap(got, "gx", gx_count, 1)
    return (got, other), offsets + [offset ^ 1 for offset in offsets]


def whole(array):
    return pl.BlockSpec(array.shape, lambda i: (0,) * array.ndim)


def update(sources, tables, first, tile_rows, inverse):
    parts = len(sources)
    held, depth, cols = sources[0].shape
    members = held * parts
    rows = ROWS
    batches, nobs = tables[0].shape[:2]
    cells = depth * cols * batches * nobs
    blocks = [pl.BlockSpec((held, rows, cols), lambda i: (0, i, 0))] * parts
    return pl.pallas_call(
        functools.partial(
            update_body, first=first, tile_rows=tile_rows, parts=parts, inverse=inverse
        ),
        grid=(depth // rows,),
        in_specs=[whole(table) for table in tables] + blocks,
        out_specs=blocks,
        out_shape=[jax.ShapeDtypeStruct((held, depth, cols), F32)] * parts,
        scratch_shapes=[pltpu.VMEM((members, rows, cols), F32)] if parts > 1 else [],
        cost_estimate=pl.CostEstimate(
            flops=cells * members * 10,
            bytes_accessed=8 * members * depth * cols,
            transcendentals=cells,
        ),
        compiler_params=LIGHT,
        name="update",
    )(*tables, *sources)


def assemble_body(whole_ref, *refs, first, tile_rows, here):
    pieces, out_ref, sems = refs[:-2], refs[-2], refs[-1]
    row_at = lax.axis_index("gx")
    copies = []
    for tile in range(whole_ref.shape[0]):
        rows = pl.ds(tile * tile_rows, first)
        copies.append(
            pltpu.make_async_copy(whole_ref.at[tile], out_ref.at[:, rows, :], sems.at[tile])
        )
    for slot, piece in enumerate(pieces):
        start = pl.multiple_of((row_at ^ slot) * tile_rows + first, here)
        rows = pl.ds(start, tile_rows - first)
        copies.append(
            pltpu.make_async_copy(
                piece, out_ref.at[:, rows, :], sems.at[whole_ref.shape[0] + slot]
            )
        )
    for copy in copies:
        copy.start()
    for copy in copies:
        copy.wait()


def local(ensemble, obs_values, obs_error, tile_weight, owner_device, obs_cells):
    gx_count = lax.axis_size("gx")
    gy_count = lax.axis_size("gy")
    held, all_rows, tile_cols = ensemble.shape
    members = held * gx_count
    tile_rows = all_rows // gx_count
    batches, nobs = obs_cells.shape
    inverse = 1.0 / (all_rows // 4)
    weight = tile_weight[:, :, 0, 0]
    payload = held * batches + len(pairs_of(batches))
    payload = -(-payload // 8) * 8
    in_smem = pl.BlockSpec(memory_space=SMEM)
    in_vmem = pl.BlockSpec(memory_space=VMEM)
    in_hbm = pl.BlockSpec(memory_space=pltpu.MemorySpace.HBM)
    geometry = dict(tile_rows=tile_rows, tile_cols=tile_cols, gy_count=gy_count, inverse=inverse)

    first = tile_rows * FIRST_EIGHTHS // 8
    rest = tile_rows - first
    picked, blocks, *pieces = pl.pallas_call(
        functools.partial(
            pick_body, tile_rows=tile_rows, first=first, gx_count=gx_count, gy_count=gy_count
        ),
        in_specs=[in_hbm] * 4,
        out_specs=[in_vmem] + [in_hbm] * (1 + gx_count),
        out_shape=[
            jax.ShapeDtypeStruct((payload, nobs), F32),
            jax.ShapeDtypeStruct((gx_count, held, first, tile_cols), F32),
        ]
        + [jax.ShapeDtypeStruct((held, rest, tile_cols), F32)] * gx_count,
        scratch_shapes=[
            pltpu.VMEM((gx_count, held, tile_rows, tile_cols), F32),
            pltpu.SMEM((batches,), jnp.int32),
            pltpu.VMEM((batches, nobs), jnp.int32),
            pltpu.VMEM((batches, nobs), F32),
            pltpu.SemaphoreType.DMA((gx_count,)),
            pltpu.SemaphoreType.DMA((2 * gx_count,)),
            pltpu.SemaphoreType.DMA((3,)),
        ],
        name="pick",
    )(owner_device, obs_cells, weight, ensemble)
    state = lax.all_to_all(blocks, "gx", split_axis=0, concat_axis=0, tiled=True)
    for slot in range(1, gx_count):
        pieces[slot] = lax.ppermute(pieces[slot], "gx", [(i, i ^ slot) for i in range(gx_count)])
    places = pl.pallas_call(
        functools.partial(tables_body, **geometry),
        in_specs=[in_smem, in_vmem],
        out_specs=[in_vmem] * 2,
        out_shape=[
            jax.ShapeDtypeStruct((batches, nobs, nobs), F32),
            jax.ShapeDtypeStruct((batches, nobs, tile_cols), F32),
        ],
        compiler_params=LIGHT,
        name="tables",
    )(owner_device, obs_cells)
    got, offsets = share(picked, gx_count, gy_count)
    wide = -(-3 * members // nobs) * nobs
    chain = pl.pallas_call(
        functools.partial(chain_body, held=held, offsets=offsets, **geometry),
        in_specs=[in_smem] + [in_vmem] * 6,
        out_specs=[in_vmem] * 2,
        out_shape=[
            jax.ShapeDtypeStruct((batches, nobs, wide), BF16),
            jax.ShapeDtypeStruct((batches, 2 * members, 2 * nobs), BF16),
        ],
        scratch_shapes=[pltpu.VMEM((batches, members, nobs), F32)],
        compiler_params=LIGHT,
        name="chain",
    )
    factors = chain(owner_device, obs_cells, obs_values, obs_error, weight, *got)
    tables = [*factors, *places]

    (upper,) = update([state.reshape(members, first, tile_cols)], tables, 0, tile_rows, inverse)
    upper = lax.all_to_all(
        upper.reshape(gx_count, held, first, tile_cols),
        "gx",
        split_axis=0,
        concat_axis=0,
        tiled=True,
    )
    lower = [*update(pieces, tables, first, tile_rows, inverse)]
    for slot in range(1, gx_count):
        lower[slot] = lax.ppermute(
            lower[slot], "gx", [(i, i ^ slot) for i in range(gx_count)]
        )
    return pl.pallas_call(
        functools.partial(assemble_body, first=first, tile_rows=tile_rows, here=ROWS),
        in_specs=[in_vmem] * (1 + gx_count),
        out_specs=in_hbm,
        out_shape=jax.ShapeDtypeStruct(ensemble.shape, F32),
        scratch_shapes=[pltpu.SemaphoreType.DMA((2 * gx_count,))],
        compiler_params=LIGHT,
        name="assemble",
    )(upper, *lower)


def solution(mesh):
    placed = (P("gx", None, "gy"), P(), P(), P(None, None, "gx", "gy"), P(), P())
    return jax.shard_map(
        local, mesh=mesh, in_specs=placed, out_specs=P("gx", None, "gy"), check_vma=False
    )
```

```python
import functools

import jax
import jax.numpy as jnp
from jax import lax
from jax.experimental import pallas as pl
from jax.experimental.pallas import tpu as pltpu
from jax.sharding import PartitionSpec as P


EPSILON = 1e-06
FIRST_EIGHTHS = 3
LIGHT = pltpu.CompilerParams(vmem_limit_bytes=16 << 20)
ROWS = 8
F32 = jnp.float32
BF16 = jnp.bfloat16
VMEM = pltpu.MemorySpace.VMEM
SMEM = pltpu.MemorySpace.SMEM


def split_two(value):
    high = value.astype(BF16)
    low = (value - high.astype(F32)).astype(BF16)
    return high, low


def pairs_of(batches):
    return [(b, later) for b in range(batches) for later in range(b + 1, batches)]


def pick_body(
    owner_in,
    cells_in,
    weight_in,
    ens_ref,
    blocks_ref,
    *refs,
    tile_rows,
    first,
    gx_count,
    gy_count,
):
    pieces = refs[:gx_count]
    window, payload_ref, owner_ref, cells_ref, weight_ref, in_sems, out_sems, small_sems = refs[
        gx_count:
    ]
    batches, nobs = cells_ref.shape
    held, _, cols = ens_ref.shape
    row_at = lax.axis_index("gx")
    col_at = lax.axis_index("gy")
    me = row_at * gy_count + col_at

    def fetch(tile):
        rows = pl.ds(tile * tile_rows, tile_rows)
        return pltpu.make_async_copy(ens_ref.at[:, rows, :], window.at[tile], in_sems.at[tile])

    def put(tile):
        other = window.at[tile, :, pl.ds(first, tile_rows - first), :]
        return pltpu.make_async_copy(other, blocks_ref.at[tile], out_sems.at[tile])

    small = [
        pltpu.make_async_copy(source, target, small_sems.at[at])
        for at, (source, target) in enumerate(
            [(owner_in, owner_ref), (cells_in, cells_ref), (weight_in, weight_ref)]
        )
    ]
    for copy in small:
        copy.start()
    for tile in range(gx_count):
        fetch(tile).start()
    payload_ref[...] = jnp.zeros_like(payload_ref)
    for copy in small:
        copy.wait()
    for at, (b, later) in enumerate(pairs_of(batches)):
        row = held * batches + at
        payload_ref[row : row + 1, :] = jnp.where(owner_ref[later] == me, weight_ref[b : b + 1, :], 0.0)
    hits = []
    for b in range(batches):
        cell = cells_ref[b : b + 1, :]
        row_hit = (lax.broadcasted_iota(jnp.int32, (tile_rows, nobs), 0) == cell // cols).astype(F32)
        row_hit = row_hit.astype(BF16)
        col_hit = lax.broadcasted_iota(jnp.int32, (cols, nobs), 0) == cell % cols
        hits.append((jnp.concatenate([row_hit] * 3, axis=0), col_hit))
    for tile in range(gx_count):
        fetch(tile).wait()
    for tile in range(gx_count):
        put(tile).start()
    for slot in range(gx_count):
        pieces[slot][:, :first, :] = window[row_at ^ slot, :, :first, :]
    for b in range(batches):
        row_hit, col_hit = hits[b]
        owner_row = owner_ref[b] // gy_count
        mine = owner_ref[b] % gy_count == col_at
        for m in range(held):
            values = window[owner_row, m]
            high = values.astype(BF16)
            rest = values - high.astype(F32)
            middle, low = split_two(rest)
            stacked = jnp.concatenate([high, middle, low], axis=0)
            columns = lax.dot_general(
                stacked, row_hit, (((0,), (0,)), ((), ())), preferred_element_type=F32
            )
            picked = jnp.sum(jnp.where(col_hit, columns, 0.0), axis=0, keepdims=True)
            row = m * batches + b
            payload_ref[row : row + 1, :] = jnp.where(mine, picked, 0.0)
    deep = payload_ref.shape[0] // held
    for slot in range(gx_count):
        pieces[slot][:, first:, :] = jnp.zeros((held, deep, cols), F32)
        for m in range(held):
            pieces[slot][m, first:, :nobs] = payload_ref[m * deep : (m + 1) * deep, :]
    for tile in range(gx_count):
        put(tile).wait()


def observed_at(owner_ref, cells_ref, b, tile_rows, tile_cols, gy_count, inverse):
    nobs = cells_ref.shape[1]
    cell = cells_ref[b : b + 1, :]
    owner = owner_ref[b]
    ox = ((owner // gy_count) * tile_rows + cell // tile_cols).astype(F32) * inverse
    oy = ((owner % gy_count) * tile_cols + cell % tile_cols).astype(F32) * inverse
    down_x = jnp.transpose(jnp.broadcast_to(ox, (nobs, nobs)))
    down_y = jnp.transpose(jnp.broadcast_to(oy, (nobs, nobs)))
    return ox, oy, down_x, down_y


def tables_body(
    owner_ref, cells_ref, x_ref, y_ref, *, tile_rows, tile_cols, gy_count, inverse
):
    batches, nobs = cells_ref.shape
    left = lax.axis_index("gy") * tile_cols
    for b in range(batches):
        _, _, down_x, down_y = observed_at(
            owner_ref, cells_ref, b, tile_rows, tile_cols, gy_count, inverse
        )
        x_ref[b] = down_x
        for piece in range(tile_cols // nobs):
            lanes = slice(piece * nobs, (piece + 1) * nobs)
            grid = lax.broadcasted_iota(jnp.int32, (nobs, nobs), 1) + (left + piece * nobs)
            away = down_y - grid.astype(F32) * inverse
            y_ref[b, :, lanes] = away * away


def chain_body(
    owner_ref,
    cells_ref,
    values_ref,
    errors_ref,
    weight_ref,
    *refs,
    tile_rows,
    tile_cols,
    held,
    gx_count,
    gy_count,
    inverse,
):
    batches, nobs = cells_ref.shape
    members = held * gx_count
    parts, (a_ref, w_ref, prior_ref) = refs[:gy_count], refs[gy_count:]
    weights = jnp.zeros(parts[0].shape[1:], F32)
    row_at = lax.axis_index("gx")
    for slot in range(gx_count):
        part = parts[0][slot]
        for other in parts[1:]:
            part = part + other[slot]
        weights = weights + part
        source = held * (row_at ^ slot)
        for m in range(held):
            for b in range(batches):
                row = m * batches + b
                prior_ref[b, pl.ds(source + m, 1), :] = part[row : row + 1, :]
    pair_weight = {
        pair: weights[held * batches + at : held * batches + at + 1, :]
        for at, pair in enumerate(pairs_of(batches))
    }
    places = [
        observed_at(owner_ref, cells_ref, b, tile_rows, tile_cols, gy_count, inverse)
        for b in range(batches)
    ]
    for b in range(batches):
        prior = prior_ref[b]
        average = jnp.mean(prior, axis=0, keepdims=True)
        anomaly = prior - average
        spread = jnp.sum(anomaly * anomaly, axis=0, keepdims=True) / (members - 1) + EPSILON
        noise = errors_ref[b : b + 1, :]
        post_var = 1.0 / (1.0 / spread + 1.0 / noise)
        post_mean = post_var * (average / spread + values_ref[b : b + 1, :] / noise)
        increment = post_mean - average + (jnp.sqrt(post_var / spread) - 1.0) * anomaly
        for later in range(b + 1, batches):
            there = prior_ref[later]
            deviation = there - jnp.mean(there, axis=0, keepdims=True)
            scaled = anomaly * (pair_weight[b, later] / spread / (members - 1))
            covariance = lax.dot_general(
                scaled,
                deviation,
                (((0,), (0,)), ((), ())),
                precision=lax.Precision.HIGHEST,
                preferred_element_type=F32,
            )
            dx = places[b][2] - places[later][0]
            dy = places[b][3] - places[later][1]
            gain = covariance / (1.0 + (dx * dx + dy * dy))
            prior_ref[later] = there + jnp.dot(
                increment, gain, precision=lax.Precision.HIGHEST, preferred_element_type=F32
            )
        scaled = anomaly * (weight_ref[b : b + 1, :] / spread / (members - 1))
        high, low = split_two(scaled)
        stacked = jnp.concatenate([high, high, low], axis=0).astype(F32)
        wide = a_ref.shape[2]
        if wide > stacked.shape[0]:
            stacked = jnp.concatenate(
                [stacked, jnp.zeros((wide - stacked.shape[0], nobs), F32)], axis=0
            )
        a_ref[b] = jnp.transpose(stacked).astype(BF16)
        high, low = split_two(increment)
        w_ref[b, :members, :nobs] = high
        w_ref[b, :members, nobs:] = high
        w_ref[b, members:, :nobs] = low
        w_ref[b, members:, nobs:] = low


def update_body(a_ref, w_ref, x_ref, y_ref, *refs, first, tile_rows, parts, inverse):
    sources, targets, scratch = refs[: parts[0]], refs[parts[0] : sum(parts)], refs[-1]
    members, rows, cols = scratch.shape
    batches, nobs, _ = x_ref.shape
    row_at = lax.axis_index("gx")
    top = row_at * tile_rows + first + pl.program_id(0) * rows
    from_ref, to_ref = sources[0], targets[0]
    if len(sources) > 1:
        from_ref = scratch
        held = members // len(sources)
        for slot, source in enumerate(sources):
            from_ref[pl.ds(held * (row_at ^ slot), held)] = source[...]
    if len(targets) > 1:
        to_ref = scratch
    states = [from_ref[:, r, :] for r in range(rows)]
    for b in range(batches):
        scaled = a_ref[b][:, : 3 * members]
        increment = w_ref[b]
        for r in range(rows):
            state = states[r]
            deviation = state - jnp.mean(state, axis=0, keepdims=True)
            high, low = split_two(deviation)
            covariance = jnp.dot(
                scaled, jnp.concatenate([high, low, high], axis=0), preferred_element_type=F32
            )
            dx = x_ref[b] - (top + r).astype(F32) * inverse
            dx = 1.0 + dx * dx
            away = jnp.concatenate([dx] * (cols // nobs), axis=1) + y_ref[b]
            gain = covariance * pl.reciprocal(away)
            high, low = split_two(gain)
            change = jnp.dot(
                increment, jnp.concatenate([high, low], axis=0), preferred_element_type=F32
            )
            states[r] = state + (change[:members] + change[members:])
    for r in range(rows):
        to_ref[:, r, :] = states[r]
    if len(targets) > 1:
        held = members // len(targets)
        for slot, target in enumerate(targets):
            target[...] = to_ref[pl.ds(held * (row_at ^ slot), held)]


def whole(array):
    return pl.BlockSpec(array.shape, lambda i: (0,) * array.ndim)


def update(sources, tables, first, depth, tile_rows, parts, inverse):
    held, _, cols = sources[0].shape
    members = held * len(sources)
    rows = ROWS
    batches, nobs = tables[0].shape[:2]
    cells = depth * cols * batches * nobs
    out = members // parts
    return pl.pallas_call(
        functools.partial(
            update_body,
            first=first,
            tile_rows=tile_rows,
            parts=(len(sources), parts),
            inverse=inverse,
        ),
        grid=(depth // rows,),
        in_specs=[whole(table) for table in tables]
        + [pl.BlockSpec((held, rows, cols), lambda i: (0, i, 0))] * len(sources),
        out_specs=[pl.BlockSpec((out, rows, cols), lambda i: (0, i, 0))] * parts,
        out_shape=[jax.ShapeDtypeStruct((out, depth, cols), F32)] * parts,
        scratch_shapes=[pltpu.VMEM((members, rows, cols), F32)],
        cost_estimate=pl.CostEstimate(
            flops=cells * members * 10,
            bytes_accessed=8 * members * depth * cols,
            transcendentals=cells,
        ),
        compiler_params=LIGHT,
        name="update",
    )(*tables, *sources)


def assemble_body(whole_ref, *refs, first, tile_rows, here):
    pieces, out_ref, sems = refs[:-2], refs[-2], refs[-1]
    row_at = lax.axis_index("gx")
    copies = []
    for tile in range(whole_ref.shape[0]):
        rows = pl.ds(tile * tile_rows, first)
        copies.append(
            pltpu.make_async_copy(whole_ref.at[tile], out_ref.at[:, rows, :], sems.at[tile])
        )
    for slot, piece in enumerate(pieces):
        start = pl.multiple_of((row_at ^ slot) * tile_rows + first, here)
        rows = pl.ds(start, tile_rows - first)
        copies.append(
            pltpu.make_async_copy(
                piece, out_ref.at[:, rows, :], sems.at[whole_ref.shape[0] + slot]
            )
        )
    for copy in copies:
        copy.start()
    for copy in copies:
        copy.wait()


def local(ensemble, obs_values, obs_error, tile_weight, owner_device, obs_cells):
    gx_count = lax.axis_size("gx")
    gy_count = lax.axis_size("gy")
    held, all_rows, tile_cols = ensemble.shape
    members = held * gx_count
    tile_rows = all_rows // gx_count
    batches, nobs = obs_cells.shape
    inverse = 1.0 / (all_rows // 4)
    weight = tile_weight[:, :, 0, 0]
    payload = held * batches + len(pairs_of(batches))
    deep = -(-payload // (8 * held)) * 8
    payload = held * deep
    in_smem = pl.BlockSpec(memory_space=SMEM)
    in_vmem = pl.BlockSpec(memory_space=VMEM)
    in_hbm = pl.BlockSpec(memory_space=pltpu.MemorySpace.HBM)
    geometry = dict(tile_rows=tile_rows, tile_cols=tile_cols, gy_count=gy_count, inverse=inverse)

    first = tile_rows * FIRST_EIGHTHS // 8
    rest = tile_rows - first
    blocks, *pieces = pl.pallas_call(
        functools.partial(
            pick_body, tile_rows=tile_rows, first=first, gx_count=gx_count, gy_count=gy_count
        ),
        in_specs=[in_hbm] * 4,
        out_specs=[in_hbm] + [in_vmem] * gx_count,
        out_shape=[jax.ShapeDtypeStruct((gx_count, held, rest, tile_cols), F32)]
        + [jax.ShapeDtypeStruct((held, first + deep, tile_cols), F32)] * gx_count,
        scratch_shapes=[
            pltpu.VMEM((gx_count, held, tile_rows, tile_cols), F32),
            pltpu.VMEM((payload, nobs), F32),
            pltpu.SMEM((batches,), jnp.int32),
            pltpu.VMEM((batches, nobs), jnp.int32),
            pltpu.VMEM((batches, nobs), F32),
            pltpu.SemaphoreType.DMA((gx_count,)),
            pltpu.SemaphoreType.DMA((gx_count,)),
            pltpu.SemaphoreType.DMA((3,)),
        ],
        name="pick",
    )(owner_device, obs_cells, weight, ensemble)
    for slot in range(1, gx_count):
        pieces[slot] = lax.ppermute(pieces[slot], "gx", [(i, i ^ slot) for i in range(gx_count)])
    state = lax.all_to_all(blocks, "gx", split_axis=0, concat_axis=0, tiled=True)
    places = pl.pallas_call(
        functools.partial(tables_body, **geometry),
        in_specs=[in_smem, in_vmem],
        out_specs=[in_vmem] * 2,
        out_shape=[
            jax.ShapeDtypeStruct((batches, nobs, nobs), F32),
            jax.ShapeDtypeStruct((batches, nobs, tile_cols), F32),
        ],
        compiler_params=LIGHT,
        name="tables",
    )(owner_device, obs_cells)
    got = [jnp.stack([piece[:, first:, :nobs].reshape(payload, nobs) for piece in pieces])]
    for step in range(1, gy_count):
        got.append(lax.ppermute(got[0], "gy", [(i, i ^ step) for i in range(gy_count)]))
    wide = -(-3 * members // nobs) * nobs
    chain = pl.pallas_call(
        functools.partial(chain_body, held=held, gx_count=gx_count, **geometry),
        in_specs=[in_smem] + [in_vmem] * (4 + gy_count),
        out_specs=[in_vmem] * 2,
        out_shape=[
            jax.ShapeDtypeStruct((batches, nobs, wide), BF16),
            jax.ShapeDtypeStruct((batches, 2 * members, 2 * nobs), BF16),
        ],
        scratch_shapes=[pltpu.VMEM((batches, members, nobs), F32)],
        compiler_params=LIGHT,
        name="chain",
    )
    factors = chain(owner_device, obs_cells, obs_values, obs_error, weight, *got)
    tables = [*factors, *places]

    (upper,) = update(pieces, tables, 0, first, tile_rows, 1, inverse)
    upper = lax.all_to_all(
        upper.reshape(gx_count, held, first, tile_cols),
        "gx",
        split_axis=0,
        concat_axis=0,
        tiled=True,
    )
    state = state.reshape(members, rest, tile_cols)
    lower = [*update([state], tables, first, rest, tile_rows, gx_count, inverse)]
    for slot in range(1, gx_count):
        lower[slot] = lax.ppermute(
            lower[slot], "gx", [(i, i ^ slot) for i in range(gx_count)]
        )
    return pl.pallas_call(
        functools.partial(assemble_body, first=first, tile_rows=tile_rows, here=ROWS),
        in_specs=[in_vmem] * (1 + gx_count),
        out_specs=in_hbm,
        out_shape=jax.ShapeDtypeStruct(ensemble.shape, F32),
        scratch_shapes=[pltpu.SemaphoreType.DMA((2 * gx_count,))],
        compiler_params=LIGHT,
        name="assemble",
    )(upper, *lower)


def solution(mesh):
    placed = (P("gx", None, "gy"), P(), P(), P(None, None, "gx", "gy"), P(), P())
    return jax.shard_map(
        local, mesh=mesh, in_specs=placed, out_specs=P("gx", None, "gy"), check_vma=False
    )
```

```python
import functools

import jax
import jax.numpy as jnp
from jax import lax
from jax.experimental import pallas as pl
from jax.experimental.pallas import tpu as pltpu
from jax.sharding import PartitionSpec as P


EPSILON = 1e-06
FIRST_EIGHTHS = 3
LIGHT = pltpu.CompilerParams(vmem_limit_bytes=16 << 20)
ROWS = 8
F32 = jnp.float32
BF16 = jnp.bfloat16
VMEM = pltpu.MemorySpace.VMEM
SMEM = pltpu.MemorySpace.SMEM


def split_two(value):
    high = value.astype(BF16)
    low = (value - high.astype(F32)).astype(BF16)
    return high, low


def pairs_of(batches):
    return [(b, later) for b in range(batches) for later in range(b + 1, batches)]


def pick_body(
    owner_in,
    cells_in,
    weight_in,
    ens_ref,
    blocks_ref,
    *refs,
    tile_rows,
    first,
    gx_count,
    gy_count,
):
    pieces = refs[:gx_count]
    window, payload_ref, owner_ref, cells_ref, weight_ref, in_sems, out_sems, small_sems = refs[
        gx_count:
    ]
    batches, nobs = cells_ref.shape
    held, _, cols = ens_ref.shape
    row_at = lax.axis_index("gx")
    col_at = lax.axis_index("gy")
    me = row_at * gy_count + col_at

    def fetch(tile):
        rows = pl.ds(tile * tile_rows, tile_rows)
        return pltpu.make_async_copy(ens_ref.at[:, rows, :], window.at[tile], in_sems.at[tile])

    def put(tile):
        other = window.at[tile, :, pl.ds(first, tile_rows - first), :]
        return pltpu.make_async_copy(other, blocks_ref.at[tile], out_sems.at[tile])

    small = [
        pltpu.make_async_copy(source, target, small_sems.at[at])
        for at, (source, target) in enumerate(
            [(owner_in, owner_ref), (cells_in, cells_ref), (weight_in, weight_ref)]
        )
    ]
    for copy in small:
        copy.start()
    for tile in range(gx_count):
        fetch(tile).start()
    payload_ref[...] = jnp.zeros_like(payload_ref)
    for copy in small:
        copy.wait()
    for at, (b, later) in enumerate(pairs_of(batches)):
        row = held * batches + at
        payload_ref[row : row + 1, :] = jnp.where(owner_ref[later] == me, weight_ref[b : b + 1, :], 0.0)
    hits = []
    for b in range(batches):
        cell = cells_ref[b : b + 1, :]
        row_hit = (lax.broadcasted_iota(jnp.int32, (tile_rows, nobs), 0) == cell // cols).astype(F32)
        row_hit = row_hit.astype(BF16)
        col_hit = lax.broadcasted_iota(jnp.int32, (cols, nobs), 0) == cell % cols
        hits.append((jnp.concatenate([row_hit] * 3, axis=0), col_hit))
    for tile in range(gx_count):
        fetch(tile).wait()
    for tile in range(gx_count):
        put(tile).start()
    folds = cols // nobs
    for slot in range(gx_count):
        for m in range(held):
            for fold in range(folds):
                at = (m * folds + fold) * first
                lanes = slice(fold * nobs, (fold + 1) * nobs)
                pieces[slot][at : at + first, :] = window[row_at ^ slot, m, :first, lanes]
    for b in range(batches):
        row_hit, col_hit = hits[b]
        owner_row = owner_ref[b] // gy_count
        mine = owner_ref[b] % gy_count == col_at
        for m in range(held):
            values = window[owner_row, m]
            high = values.astype(BF16)
            rest = values - high.astype(F32)
            middle, low = split_two(rest)
            stacked = jnp.concatenate([high, middle, low], axis=0)
            columns = lax.dot_general(
                stacked, row_hit, (((0,), (0,)), ((), ())), preferred_element_type=F32
            )
            picked = jnp.sum(jnp.where(col_hit, columns, 0.0), axis=0, keepdims=True)
            row = m * batches + b
            payload_ref[row : row + 1, :] = jnp.where(mine, picked, 0.0)
    for slot in range(gx_count):
        pieces[slot][held * folds * first :, :] = payload_ref[...]
    for tile in range(gx_count):
        put(tile).wait()


def observed_at(owner_ref, cells_ref, b, tile_rows, tile_cols, gy_count, inverse):
    nobs = cells_ref.shape[1]
    cell = cells_ref[b : b + 1, :]
    owner = owner_ref[b]
    ox = ((owner // gy_count) * tile_rows + cell // tile_cols).astype(F32) * inverse
    oy = ((owner % gy_count) * tile_cols + cell % tile_cols).astype(F32) * inverse
    down_x = jnp.transpose(jnp.broadcast_to(ox, (nobs, nobs)))
    down_y = jnp.transpose(jnp.broadcast_to(oy, (nobs, nobs)))
    return ox, oy, down_x, down_y


def tables_body(
    owner_ref, cells_ref, x_ref, y_ref, taper_ref, *, tile_rows, tile_cols, gy_count, inverse
):
    batches, nobs = cells_ref.shape
    left = lax.axis_index("gy") * tile_cols
    places = [
        observed_at(owner_ref, cells_ref, b, tile_rows, tile_cols, gy_count, inverse)
        for b in range(batches)
    ]
    for b, (_, _, down_x, down_y) in enumerate(places):
        x_ref[b] = down_x
        for piece in range(tile_cols // nobs):
            lanes = slice(piece * nobs, (piece + 1) * nobs)
            grid = lax.broadcasted_iota(jnp.int32, (nobs, nobs), 1) + (left + piece * nobs)
            away = down_y - grid.astype(F32) * inverse
            y_ref[b, :, lanes] = away * away
    for at, (b, later) in enumerate(pairs_of(batches)):
        dx = places[b][2] - places[later][0]
        dy = places[b][3] - places[later][1]
        taper_ref[at] = pl.reciprocal(1.0 + (dx * dx + dy * dy))


def factor_rows(increment):
    high, low = split_two(increment)
    return jnp.concatenate(
        [jnp.concatenate([high, high], axis=1), jnp.concatenate([low, low], axis=1)], axis=0
    )


def chain_body(
    values_ref, errors_ref, weight_ref, taper_ref, *refs, held, gx_count, gy_count
):
    batches, nobs = values_ref.shape
    members = held * gx_count
    parts, (a_ref, w_ref, prior_ref) = refs[:gy_count], refs[gy_count:]
    weights = jnp.zeros(parts[0].shape[1:], F32)
    row_at = lax.axis_index("gx")
    for slot in range(gx_count):
        part = parts[0][slot]
        for other in parts[1:]:
            part = part + other[slot]
        weights = weights + part
        source = held * (row_at ^ slot)
        for m in range(held):
            for b in range(batches):
                row = m * batches + b
                prior_ref[b, pl.ds(source + m, 1), :] = part[row : row + 1, :]
    for b in range(batches):
        prior = prior_ref[b]
        average = jnp.mean(prior, axis=0, keepdims=True)
        anomaly = prior - average
        spread = jnp.sum(anomaly * anomaly, axis=0, keepdims=True) / (members - 1) + EPSILON
        scaled = anomaly / (spread * (members - 1))
        high, low = split_two(scaled)
        stacked = jnp.concatenate([high, high, low], axis=0).astype(F32)
        wide = a_ref.shape[2]
        if wide > stacked.shape[0]:
            stacked = jnp.concatenate(
                [stacked, jnp.zeros((wide - stacked.shape[0], nobs), F32)], axis=0
            )
        upright = jnp.transpose(stacked).astype(BF16)
        a_ref[b] = upright
        noise = errors_ref[b : b + 1, :]
        post_var = 1.0 / (1.0 / spread + 1.0 / noise)
        post_mean = post_var * (average / spread + values_ref[b : b + 1, :] / noise)
        increment = post_mean - average + (jnp.sqrt(post_var / spread) - 1.0) * anomaly
        w_ref[b] = factor_rows(increment * weight_ref[b : b + 1, :])
        for at, (earlier, later) in enumerate(pairs_of(batches)):
            if earlier != b:
                continue
            there = prior_ref[later]
            deviation = there - jnp.mean(there, axis=0, keepdims=True)
            high, low = split_two(deviation)
            covariance = jnp.dot(
                upright[:, : 3 * members],
                jnp.concatenate([high, low, high], axis=0),
                preferred_element_type=F32,
            )
            high, low = split_two(covariance * taper_ref[at])
            row = held * batches + at
            change = jnp.dot(
                factor_rows(increment * weights[row : row + 1, :]),
                jnp.concatenate([high, low], axis=0),
                preferred_element_type=F32,
            )
            prior_ref[later] = there + (change[:members] + change[members:])


def update_body(
    a_ref, w_ref, x_ref, y_ref, *refs, first, depth, tile_rows, parts, inverse
):
    sources, targets, scratch = refs[: parts[0]], refs[parts[0] : sum(parts)], refs[-1]
    members, rows, cols = scratch.shape
    batches, nobs, _ = x_ref.shape
    row_at = lax.axis_index("gx")
    top = row_at * tile_rows + first + pl.program_id(0) * rows
    from_ref, to_ref = sources[0], targets[0]
    if len(sources) > 1:
        from_ref = scratch
        held = members // len(sources)
        folds = cols // nobs
        for slot, source in enumerate(sources):
            for m in range(held):
                for fold in range(folds):
                    at = (m * folds + fold) * depth + pl.program_id(0) * rows
                    lanes = slice(fold * nobs, (fold + 1) * nobs)
                    from_ref[held * (row_at ^ slot) + m, :, lanes] = source[
                        pl.ds(pl.multiple_of(at, rows), rows), :
                    ]
    if len(targets) > 1:
        to_ref = scratch
    states = [from_ref[:, r, :] for r in range(rows)]
    for b in range(batches):
        scaled = a_ref[b][:, : 3 * members]
        increment = w_ref[b]
        for r in range(rows):
            state = states[r]
            deviation = state - jnp.mean(state, axis=0, keepdims=True)
            high, low = split_two(deviation)
            covariance = jnp.dot(
                scaled, jnp.concatenate([high, low, high], axis=0), preferred_element_type=F32
            )
            dx = x_ref[b] - (top + r).astype(F32) * inverse
            dx = 1.0 + dx * dx
            away = jnp.concatenate([dx] * (cols // nobs), axis=1) + y_ref[b]
            gain = covariance * pl.reciprocal(away)
            high, low = split_two(gain)
            change = jnp.dot(
                increment, jnp.concatenate([high, low], axis=0), preferred_element_type=F32
            )
            states[r] = state + (change[:members] + change[members:])
    for r in range(rows):
        to_ref[:, r, :] = states[r]
    if len(targets) > 1:
        held = members // len(targets)
        for slot, target in enumerate(targets):
            target[...] = to_ref[pl.ds(held * (row_at ^ slot), held)]


def whole(array):
    return pl.BlockSpec(array.shape, lambda i: (0,) * array.ndim)


def update(sources, tables, first, depth, tile_rows, tile_cols, members, parts, inverse):
    rows, cols = ROWS, tile_cols
    batches, nobs = tables[0].shape[:2]
    cells = depth * cols * batches * nobs
    out = members // parts
    return pl.pallas_call(
        functools.partial(
            update_body,
            first=first,
            depth=depth,
            tile_rows=tile_rows,
            parts=(len(sources), parts),
            inverse=inverse,
        ),
        grid=(depth // rows,),
        in_specs=[whole(table) for table in tables]
        + (
            [whole(source) for source in sources]
            if len(sources) > 1
            else [pl.BlockSpec((members, rows, cols), lambda i: (0, i, 0))]
        ),
        out_specs=[pl.BlockSpec((out, rows, cols), lambda i: (0, i, 0))] * parts,
        out_shape=[jax.ShapeDtypeStruct((out, depth, cols), F32)] * parts,
        scratch_shapes=[pltpu.VMEM((members, rows, cols), F32)],
        cost_estimate=pl.CostEstimate(
            flops=cells * members * 10,
            bytes_accessed=8 * members * depth * cols,
            transcendentals=cells,
        ),
        compiler_params=LIGHT,
        name="update",
    )(*tables, *sources)


def assemble_body(whole_ref, *refs, first, tile_rows, here):
    pieces, out_ref, sems = refs[:-2], refs[-2], refs[-1]
    row_at = lax.axis_index("gx")
    copies = []
    for tile in range(whole_ref.shape[0]):
        rows = pl.ds(tile * tile_rows, first)
        copies.append(
            pltpu.make_async_copy(whole_ref.at[tile], out_ref.at[:, rows, :], sems.at[tile])
        )
    for slot, piece in enumerate(pieces):
        start = pl.multiple_of((row_at ^ slot) * tile_rows + first, here)
        rows = pl.ds(start, tile_rows - first)
        copies.append(
            pltpu.make_async_copy(
                piece, out_ref.at[:, rows, :], sems.at[whole_ref.shape[0] + slot]
            )
        )
    for copy in copies:
        copy.start()
    for copy in copies:
        copy.wait()


def local(ensemble, obs_values, obs_error, tile_weight, owner_device, obs_cells):
    gx_count = lax.axis_size("gx")
    gy_count = lax.axis_size("gy")
    held, all_rows, tile_cols = ensemble.shape
    members = held * gx_count
    tile_rows = all_rows // gx_count
    batches, nobs = obs_cells.shape
    first = tile_rows * FIRST_EIGHTHS // 8
    rest = tile_rows - first
    inverse = 1.0 / (all_rows // 4)
    weight = tile_weight[:, :, 0, 0]
    payload = held * batches + len(pairs_of(batches))
    payload = -(-payload // 8) * 8
    state_rows = held * (tile_cols // nobs) * first
    in_smem = pl.BlockSpec(memory_space=SMEM)
    in_vmem = pl.BlockSpec(memory_space=VMEM)
    in_hbm = pl.BlockSpec(memory_space=pltpu.MemorySpace.HBM)
    geometry = dict(tile_rows=tile_rows, tile_cols=tile_cols, gy_count=gy_count, inverse=inverse)

    blocks, *pieces = pl.pallas_call(
        functools.partial(
            pick_body, tile_rows=tile_rows, first=first, gx_count=gx_count, gy_count=gy_count
        ),
        in_specs=[in_hbm] * 4,
        out_specs=[in_hbm] + [in_vmem] * gx_count,
        out_shape=[jax.ShapeDtypeStruct((gx_count, held, rest, tile_cols), F32)]
        + [jax.ShapeDtypeStruct((state_rows + payload, nobs), F32)] * gx_count,
        scratch_shapes=[
            pltpu.VMEM((gx_count, held, tile_rows, tile_cols), F32),
            pltpu.VMEM((payload, nobs), F32),
            pltpu.SMEM((batches,), jnp.int32),
            pltpu.VMEM((batches, nobs), jnp.int32),
            pltpu.VMEM((batches, nobs), F32),
            pltpu.SemaphoreType.DMA((gx_count,)),
            pltpu.SemaphoreType.DMA((gx_count,)),
            pltpu.SemaphoreType.DMA((3,)),
        ],
        name="pick",
    )(owner_device, obs_cells, weight, ensemble)
    for slot in range(1, gx_count):
        pieces[slot] = lax.ppermute(pieces[slot], "gx", [(i, i ^ slot) for i in range(gx_count)])
    state = lax.all_to_all(blocks, "gx", split_axis=0, concat_axis=0, tiled=True)
    *places, tapers = pl.pallas_call(
        functools.partial(tables_body, **geometry),
        in_specs=[in_smem, in_vmem],
        out_specs=[in_vmem] * 3,
        out_shape=[
            jax.ShapeDtypeStruct((batches, nobs, nobs), F32),
            jax.ShapeDtypeStruct((batches, nobs, tile_cols), F32),
            jax.ShapeDtypeStruct((len(pairs_of(batches)), nobs, nobs), F32),
        ],
        compiler_params=LIGHT,
        name="tables",
    )(owner_device, obs_cells)
    got = [jnp.stack([piece[state_rows:] for piece in pieces])]
    for step in range(1, gy_count):
        got.append(lax.ppermute(got[0], "gy", [(i, i ^ step) for i in range(gy_count)]))
    wide = -(-3 * members // nobs) * nobs
    chain = pl.pallas_call(
        functools.partial(chain_body, held=held, gx_count=gx_count, gy_count=gy_count),
        in_specs=[in_vmem] * (4 + gy_count),
        out_specs=[in_vmem] * 2,
        out_shape=[
            jax.ShapeDtypeStruct((batches, nobs, wide), BF16),
            jax.ShapeDtypeStruct((batches, 2 * members, 2 * nobs), BF16),
        ],
        scratch_shapes=[pltpu.VMEM((batches, members, nobs), F32)],
        compiler_params=LIGHT,
        name="chain",
    )
    factors = chain(obs_values, obs_error, weight, tapers, *got)
    tables = [*factors, *places]

    shape = (tile_rows, tile_cols, members)
    (upper,) = update(pieces, tables, 0, first, *shape, 1, inverse)
    upper = lax.all_to_all(
        upper.reshape(gx_count, held, first, tile_cols),
        "gx",
        split_axis=0,
        concat_axis=0,
        tiled=True,
    )
    state = state.reshape(members, rest, tile_cols)
    lower = [*update([state], tables, first, rest, *shape, gx_count, inverse)]
    for slot in range(1, gx_count):
        lower[slot] = lax.ppermute(
            lower[slot], "gx", [(i, i ^ slot) for i in range(gx_count)]
        )
    return pl.pallas_call(
        functools.partial(assemble_body, first=first, tile_rows=tile_rows, here=ROWS),
        in_specs=[in_vmem] * (1 + gx_count),
        out_specs=in_hbm,
        out_shape=jax.ShapeDtypeStruct(ensemble.shape, F32),
        scratch_shapes=[pltpu.SemaphoreType.DMA((2 * gx_count,))],
        compiler_params=LIGHT,
        name="assemble",
    )(upper, *lower)


def solution(mesh):
    placed = (P("gx", None, "gy"), P(), P(), P(None, None, "gx", "gy"), P(), P())
    return jax.shard_map(
        local, mesh=mesh, in_specs=placed, out_specs=P("gx", None, "gy"), check_vma=False
    )
```

```python
import functools

import jax
import jax.numpy as jnp
from jax import lax
from jax.experimental import pallas as pl
from jax.experimental.pallas import tpu as pltpu
from jax.sharding import PartitionSpec as P


EPSILON = 1e-06
IN_EIGHTHS = 4
OUT_EIGHTHS = 3
LIGHT = pltpu.CompilerParams(vmem_limit_bytes=16 << 20)
ROWS = 8
F32 = jnp.float32
BF16 = jnp.bfloat16
VMEM = pltpu.MemorySpace.VMEM
SMEM = pltpu.MemorySpace.SMEM


def split_two(value):
    high = value.astype(BF16)
    low = (value - high.astype(F32)).astype(BF16)
    return high, low


def pairs_of(batches):
    return [(b, later) for b in range(batches) for later in range(b + 1, batches)]


def pick_body(
    owner_in,
    cells_in,
    weight_in,
    ens_ref,
    blocks_ref,
    *refs,
    tile_rows,
    first,
    gx_count,
    gy_count,
):
    pieces = refs[:gx_count]
    window, payload_ref, owner_ref, cells_ref, weight_ref, in_sems, out_sems, small_sems = refs[
        gx_count:
    ]
    batches, nobs = cells_ref.shape
    held, _, cols = ens_ref.shape
    row_at = lax.axis_index("gx")
    col_at = lax.axis_index("gy")
    me = row_at * gy_count + col_at

    def fetch(tile):
        rows = pl.ds(tile * tile_rows, tile_rows)
        return pltpu.make_async_copy(ens_ref.at[:, rows, :], window.at[tile], in_sems.at[tile])

    def put(tile):
        other = window.at[tile, :, pl.ds(first, tile_rows - first), :]
        return pltpu.make_async_copy(other, blocks_ref.at[tile], out_sems.at[tile])

    small = [
        pltpu.make_async_copy(source, target, small_sems.at[at])
        for at, (source, target) in enumerate(
            [(owner_in, owner_ref), (cells_in, cells_ref), (weight_in, weight_ref)]
        )
    ]
    for copy in small:
        copy.start()
    for tile in range(gx_count):
        fetch(tile).start()
    payload_ref[...] = jnp.zeros_like(payload_ref)
    for copy in small:
        copy.wait()
    pairs_at = -(-held * batches // 8) * 8
    for at, (b, later) in enumerate(pairs_of(batches)):
        row = pairs_at + at
        payload_ref[row : row + 1, :] = jnp.where(owner_ref[later] == me, weight_ref[b : b + 1, :], 0.0)
    hits = []
    for b in range(batches):
        cell = cells_ref[b : b + 1, :]
        row_hit = (lax.broadcasted_iota(jnp.int32, (tile_rows, nobs), 0) == cell // cols).astype(F32)
        row_hit = row_hit.astype(BF16)
        col_hit = lax.broadcasted_iota(jnp.int32, (cols, nobs), 0) == cell % cols
        hits.append((jnp.concatenate([row_hit] * 3, axis=0), col_hit))
    for tile in range(gx_count):
        fetch(tile).wait()
    for tile in range(gx_count):
        put(tile).start()
    folds = cols // nobs
    for slot in range(gx_count):
        for m in range(held):
            for fold in range(folds):
                at = (m * folds + fold) * first
                lanes = slice(fold * nobs, (fold + 1) * nobs)
                pieces[slot][at : at + first, :] = window[row_at ^ slot, m, :first, lanes]
    for b in range(batches):
        row_hit, col_hit = hits[b]
        owner_row = owner_ref[b] // gy_count
        mine = owner_ref[b] % gy_count == col_at
        for m in range(held):
            values = window[owner_row, m]
            high = values.astype(BF16)
            rest = values - high.astype(F32)
            middle, low = split_two(rest)
            stacked = jnp.concatenate([high, middle, low], axis=0)
            columns = lax.dot_general(
                stacked, row_hit, (((0,), (0,)), ((), ())), preferred_element_type=F32
            )
            picked = jnp.sum(jnp.where(col_hit, columns, 0.0), axis=0, keepdims=True)
            row = m * batches + b
            payload_ref[row : row + 1, :] = jnp.where(mine, picked, 0.0)
    for slot in range(gx_count):
        pieces[slot][held * folds * first :, :] = payload_ref[...]
    for tile in range(gx_count):
        put(tile).wait()


def observed_at(owner_ref, cells_ref, b, tile_rows, tile_cols, gy_count, inverse):
    nobs = cells_ref.shape[1]
    cell = cells_ref[b : b + 1, :]
    owner = owner_ref[b]
    ox = ((owner // gy_count) * tile_rows + cell // tile_cols).astype(F32) * inverse
    oy = ((owner % gy_count) * tile_cols + cell % tile_cols).astype(F32) * inverse
    down_x = jnp.transpose(jnp.broadcast_to(ox, (nobs, nobs)))
    down_y = jnp.transpose(jnp.broadcast_to(oy, (nobs, nobs)))
    return ox, oy, down_x, down_y


def tables_body(
    owner_ref, cells_ref, x_ref, y_ref, taper_ref, *, tile_rows, tile_cols, gy_count, inverse
):
    batches, nobs = cells_ref.shape
    left = lax.axis_index("gy") * tile_cols
    places = [
        observed_at(owner_ref, cells_ref, b, tile_rows, tile_cols, gy_count, inverse)
        for b in range(batches)
    ]
    for b, (_, _, down_x, down_y) in enumerate(places):
        x_ref[b] = down_x
        for piece in range(tile_cols // nobs):
            lanes = slice(piece * nobs, (piece + 1) * nobs)
            grid = lax.broadcasted_iota(jnp.int32, (nobs, nobs), 1) + (left + piece * nobs)
            away = down_y - grid.astype(F32) * inverse
            y_ref[b, :, lanes] = away * away
    for at, (b, later) in enumerate(pairs_of(batches)):
        dx = places[b][2] - places[later][0]
        dy = places[b][3] - places[later][1]
        taper_ref[at] = pl.reciprocal(1.0 + (dx * dx + dy * dy))


def merge_body(*refs, base, picks):
    pieces, out_ref = refs[:-1], refs[-1]
    total = None
    for slot, piece in enumerate(pieces):
        out_ref[slot * picks : (slot + 1) * picks, :] = piece[base : base + picks, :]
        weights = piece[base + picks :, :]
        total = weights if total is None else total + weights
    out_ref[len(pieces) * picks :, :] = total


def factor_rows(increment):
    high, low = split_two(increment)
    return jnp.concatenate(
        [jnp.concatenate([high, high], axis=1), jnp.concatenate([low, low], axis=1)], axis=0
    )


def chain_body(
    values_ref, errors_ref, weight_ref, taper_ref, *refs, held, gx_count, gy_count
):
    batches, nobs = values_ref.shape
    members = held * gx_count
    parts, (a_ref, w_ref, prior_ref) = refs[:gy_count], refs[gy_count:]
    row_at = lax.axis_index("gx")
    picks = -(-held * batches // 8) * 8

    def total(first, count):
        rows = [part[first : first + count, :] for part in parts]
        return sum(rows[1:], rows[0])

    for slot in range(gx_count):
        part = total(slot * picks, picks)
        source = held * (row_at ^ slot)
        for m in range(held):
            for b in range(batches):
                row = m * batches + b
                prior_ref[b, pl.ds(source + m, 1), :] = part[row : row + 1, :]
    weights = total(gx_count * picks, parts[0].shape[0] - gx_count * picks)
    for b in range(batches):
        prior = prior_ref[b]
        average = jnp.mean(prior, axis=0, keepdims=True)
        anomaly = prior - average
        spread = jnp.sum(anomaly * anomaly, axis=0, keepdims=True) / (members - 1) + EPSILON
        scaled = anomaly / (spread * (members - 1))
        high, low = split_two(scaled)
        stacked = jnp.concatenate([high, high, low], axis=0).astype(F32)
        wide = a_ref.shape[2]
        if wide > stacked.shape[0]:
            stacked = jnp.concatenate(
                [stacked, jnp.zeros((wide - stacked.shape[0], nobs), F32)], axis=0
            )
        upright = jnp.transpose(stacked).astype(BF16)
        a_ref[b] = upright
        noise = errors_ref[b : b + 1, :]
        post_var = 1.0 / (1.0 / spread + 1.0 / noise)
        post_mean = post_var * (average / spread + values_ref[b : b + 1, :] / noise)
        increment = post_mean - average + (jnp.sqrt(post_var / spread) - 1.0) * anomaly
        w_ref[b] = factor_rows(increment * weight_ref[b : b + 1, :])
        for at, (earlier, later) in enumerate(pairs_of(batches)):
            if earlier != b:
                continue
            there = prior_ref[later]
            deviation = there - jnp.mean(there, axis=0, keepdims=True)
            high, low = split_two(deviation)
            covariance = jnp.dot(
                upright[:, : 3 * members],
                jnp.concatenate([high, low, high], axis=0),
                preferred_element_type=F32,
            )
            high, low = split_two(covariance * taper_ref[at])
            change = jnp.dot(
                factor_rows(increment * weights[at : at + 1, :]),
                jnp.concatenate([high, low], axis=0),
                preferred_element_type=F32,
            )
            prior_ref[later] = there + (change[:members] + change[members:])


def update_body(a_ref, w_ref, x_ref, y_ref, *refs, first, depth, tile_rows, parts, inverse):
    gx_count, ins, outs = parts
    pieces, others, targets = refs[:gx_count], refs[gx_count:ins], refs[ins : ins + outs]
    scratch = refs[-1]
    members, rows, cols = scratch.shape
    held = members // gx_count
    batches, nobs, _ = x_ref.shape
    row_at = lax.axis_index("gx")
    begin = first + pl.program_id(0) * rows
    top = row_at * tile_rows + begin
    from_ref, to_ref = scratch, targets[0]

    def unpack():
        for slot, piece in enumerate(pieces):
            for m in range(held):
                for fold in range(cols // nobs):
                    at = (m * (cols // nobs) + fold) * depth + begin
                    lanes = slice(fold * nobs, (fold + 1) * nobs)
                    from_ref[held * (row_at ^ slot) + m, :, lanes] = piece[
                        pl.ds(pl.multiple_of(at, ROWS), rows), :
                    ]

    if others:
        pl.when(begin < depth)(unpack)

        @pl.when(begin >= depth)
        def _():
            from_ref[...] = others[0][...]
    else:
        unpack()
    if len(targets) > 1:
        to_ref = scratch
    states = [from_ref[:, r, :] for r in range(rows)]
    for b in range(batches):
        scaled = a_ref[b][:, : 3 * members]
        increment = w_ref[b]
        for r in range(rows):
            state = states[r]
            deviation = state - jnp.mean(state, axis=0, keepdims=True)
            high, low = split_two(deviation)
            covariance = jnp.dot(
                scaled, jnp.concatenate([high, low, high], axis=0), preferred_element_type=F32
            )
            dx = x_ref[b] - (top + r).astype(F32) * inverse
            dx = 1.0 + dx * dx
            away = jnp.concatenate([dx] * (cols // nobs), axis=1) + y_ref[b]
            gain = covariance * pl.reciprocal(away)
            high, low = split_two(gain)
            change = jnp.dot(
                increment, jnp.concatenate([high, low], axis=0), preferred_element_type=F32
            )
            states[r] = state + (change[:members] + change[members:])
    for r in range(rows):
        to_ref[:, r, :] = states[r]
    if len(targets) > 1:
        for slot, target in enumerate(targets):
            target[...] = to_ref[pl.ds(held * (row_at ^ slot), held)]


def whole(array):
    return pl.BlockSpec(array.shape, lambda i: (0,) * array.ndim)


def update(pieces, others, tables, first, count, depth, tile_rows, cols, outs, inverse):
    gx_count = len(pieces)
    batches, nobs, _ = tables[2].shape
    members = tables[1].shape[1] // 2
    rows = count if not others else ROWS
    cells = count * cols * batches * nobs
    out = members // outs
    return pl.pallas_call(
        functools.partial(
            update_body,
            first=first,
            depth=depth,
            tile_rows=tile_rows,
            parts=(gx_count, gx_count + len(others), outs),
            inverse=inverse,
        ),
        grid=(count // rows,),
        in_specs=[whole(array) for array in (*tables, *pieces)]
        + [
            pl.BlockSpec(
                (members, rows, cols),
                lambda i: (0, jnp.maximum(i - (depth - first) // rows, 0), 0),
            )
        ]
        * len(others),
        out_specs=[pl.BlockSpec((out, rows, cols), lambda i: (0, i, 0))] * outs,
        out_shape=[jax.ShapeDtypeStruct((out, count, cols), F32)] * outs,
        scratch_shapes=[pltpu.VMEM((members, rows, cols), F32)],
        cost_estimate=pl.CostEstimate(
            flops=cells * members * 10,
            bytes_accessed=8 * members * count * cols,
            transcendentals=cells,
        ),
        compiler_params=LIGHT,
        name="update",
    )(*tables, *pieces, *others)


def assemble_body(whole_ref, *refs, first, tile_rows, here):
    pieces, out_ref, sems = refs[:-2], refs[-2], refs[-1]
    row_at = lax.axis_index("gx")
    copies = []
    for tile in range(whole_ref.shape[0]):
        rows = pl.ds(tile * tile_rows, first)
        copies.append(
            pltpu.make_async_copy(whole_ref.at[tile], out_ref.at[:, rows, :], sems.at[tile])
        )
    for slot, piece in enumerate(pieces):
        start = pl.multiple_of((row_at ^ slot) * tile_rows + first, here)
        rows = pl.ds(start, tile_rows - first)
        copies.append(
            pltpu.make_async_copy(
                piece, out_ref.at[:, rows, :], sems.at[whole_ref.shape[0] + slot]
            )
        )
    for copy in copies:
        copy.start()
    for copy in copies:
        copy.wait()


def local(ensemble, obs_values, obs_error, tile_weight, owner_device, obs_cells):
    gx_count = lax.axis_size("gx")
    gy_count = lax.axis_size("gy")
    held, all_rows, tile_cols = ensemble.shape
    members = held * gx_count
    tile_rows = all_rows // gx_count
    batches, nobs = obs_cells.shape
    first = tile_rows * IN_EIGHTHS // 8
    rest = tile_rows - first
    early = tile_rows * OUT_EIGHTHS // 8
    inverse = 1.0 / (all_rows // 4)
    weight = tile_weight[:, :, 0, 0]
    picks, pairs = [-(-n // 8) * 8 for n in (held * batches, len(pairs_of(batches)))]
    payload = picks + pairs
    state_rows = held * (tile_cols // nobs) * first
    in_smem = pl.BlockSpec(memory_space=SMEM)
    in_vmem = pl.BlockSpec(memory_space=VMEM)
    in_hbm = pl.BlockSpec(memory_space=pltpu.MemorySpace.HBM)
    geometry = dict(tile_rows=tile_rows, tile_cols=tile_cols, gy_count=gy_count, inverse=inverse)

    blocks, *pieces = pl.pallas_call(
        functools.partial(
            pick_body, tile_rows=tile_rows, first=first, gx_count=gx_count, gy_count=gy_count
        ),
        in_specs=[in_hbm] * 4,
        out_specs=[in_hbm] + [in_vmem] * gx_count,
        out_shape=[jax.ShapeDtypeStruct((gx_count, held, rest, tile_cols), F32)]
        + [jax.ShapeDtypeStruct((state_rows + payload, nobs), F32)] * gx_count,
        scratch_shapes=[
            pltpu.VMEM((gx_count, held, tile_rows, tile_cols), F32),
            pltpu.VMEM((payload, nobs), F32),
            pltpu.SMEM((batches,), jnp.int32),
            pltpu.VMEM((batches, nobs), jnp.int32),
            pltpu.VMEM((batches, nobs), F32),
            pltpu.SemaphoreType.DMA((gx_count,)),
            pltpu.SemaphoreType.DMA((gx_count,)),
            pltpu.SemaphoreType.DMA((3,)),
        ],
        name="pick",
    )(owner_device, obs_cells, weight, ensemble)
    for slot in range(1, gx_count):
        pieces[slot] = lax.ppermute(pieces[slot], "gx", [(i, i ^ slot) for i in range(gx_count)])
    state = lax.all_to_all(blocks, "gx", split_axis=0, concat_axis=0, tiled=True)
    *places, tapers = pl.pallas_call(
        functools.partial(tables_body, **geometry),
        in_specs=[in_smem, in_vmem],
        out_specs=[in_vmem] * 3,
        out_shape=[
            jax.ShapeDtypeStruct((batches, nobs, nobs), F32),
            jax.ShapeDtypeStruct((batches, nobs, tile_cols), F32),
            jax.ShapeDtypeStruct((len(pairs_of(batches)), nobs, nobs), F32),
        ],
        compiler_params=LIGHT,
        name="tables",
    )(owner_device, obs_cells)
    merge = pl.pallas_call(
        functools.partial(merge_body, base=state_rows, picks=picks),
        in_specs=[in_vmem] * gx_count,
        out_specs=in_vmem,
        out_shape=jax.ShapeDtypeStruct((gx_count * picks + pairs, nobs), F32),
        compiler_params=LIGHT,
        name="merge",
    )
    got = [merge(*pieces)]
    for step in range(1, gy_count):
        got.append(lax.ppermute(got[0], "gy", [(i, i ^ step) for i in range(gy_count)]))
    wide = -(-3 * members // nobs) * nobs
    chain = pl.pallas_call(
        functools.partial(chain_body, held=held, gx_count=gx_count, gy_count=gy_count),
        in_specs=[in_vmem] * (4 + gy_count),
        out_specs=[in_vmem] * 2,
        out_shape=[
            jax.ShapeDtypeStruct((batches, nobs, wide), BF16),
            jax.ShapeDtypeStruct((batches, 2 * members, 2 * nobs), BF16),
        ],
        scratch_shapes=[pltpu.VMEM((batches, members, nobs), F32)],
        compiler_params=LIGHT,
        name="chain",
    )
    factors = chain(obs_values, obs_error, weight, tapers, *got)
    tables = [*factors, *places]

    shape = (first, tile_rows, tile_cols)
    (upper,) = update(pieces, [], tables, 0, early, *shape, 1, inverse)
    upper = lax.all_to_all(
        upper.reshape(gx_count, held, early, tile_cols),
        "gx",
        split_axis=0,
        concat_axis=0,
        tiled=True,
    )
    state = state.reshape(members, rest, tile_cols)
    lower = [
        *update(
            pieces, [state], tables, early, tile_rows - early, *shape, gx_count, inverse
        )
    ]
    for slot in range(1, gx_count):
        lower[slot] = lax.ppermute(
            lower[slot], "gx", [(i, i ^ slot) for i in range(gx_count)]
        )
    return pl.pallas_call(
        functools.partial(assemble_body, first=early, tile_rows=tile_rows, here=ROWS),
        in_specs=[in_vmem] * (1 + gx_count),
        out_specs=in_hbm,
        out_shape=jax.ShapeDtypeStruct(ensemble.shape, F32),
        scratch_shapes=[pltpu.SemaphoreType.DMA((2 * gx_count,))],
        compiler_params=LIGHT,
        name="assemble",
    )(upper, *lower)


def solution(mesh):
    placed = (P("gx", None, "gy"), P(), P(), P(None, None, "gx", "gy"), P(), P())
    return jax.shard_map(
        local, mesh=mesh, in_specs=placed, out_specs=P("gx", None, "gy"), check_vma=False
    )
```

```python
import functools

import jax
import jax.numpy as jnp
from jax import lax
from jax.experimental import pallas as pl
from jax.experimental.pallas import tpu as pltpu
from jax.sharding import PartitionSpec as P


EPSILON = 1e-06
IN_EIGHTHS = 4
OUT_EIGHTHS = 3
LIGHT = pltpu.CompilerParams(vmem_limit_bytes=16 << 20)
SPREAD = pltpu.CompilerParams(vmem_limit_bytes=16 << 20)
ROWS = 8
F32 = jnp.float32
BF16 = jnp.bfloat16
VMEM = pltpu.MemorySpace.VMEM
SMEM = pltpu.MemorySpace.SMEM


def split_two(value):
    high = value.astype(BF16)
    low = (value - high.astype(F32)).astype(BF16)
    return high, low


def pairs_of(batches):
    return [(b, later) for b in range(batches) for later in range(b + 1, batches)]


def pick_body(
    owner_in,
    cells_in,
    weight_in,
    ens_ref,
    blocks_ref,
    *refs,
    tile_rows,
    first,
    gx_count,
    gy_count,
):
    pieces = refs[:gx_count]
    window, payload_ref, owner_ref, cells_ref, weight_ref, in_sems, out_sems, small_sems = refs[
        gx_count:
    ]
    batches, nobs = cells_ref.shape
    held, _, cols = ens_ref.shape
    row_at = lax.axis_index("gx")
    col_at = lax.axis_index("gy")
    me = row_at * gy_count + col_at

    def fetch(tile):
        rows = pl.ds(tile * tile_rows, tile_rows)
        return pltpu.make_async_copy(ens_ref.at[:, rows, :], window.at[tile], in_sems.at[tile])

    def put(tile):
        other = window.at[tile, :, pl.ds(first, tile_rows - first), :]
        return pltpu.make_async_copy(other, blocks_ref.at[tile], out_sems.at[tile])

    small = [
        pltpu.make_async_copy(source, target, small_sems.at[at])
        for at, (source, target) in enumerate(
            [(owner_in, owner_ref), (cells_in, cells_ref), (weight_in, weight_ref)]
        )
    ]
    for copy in small:
        copy.start()
    for tile in range(gx_count):
        fetch(tile).start()
    payload_ref[...] = jnp.zeros_like(payload_ref)
    for copy in small:
        copy.wait()
    pairs_at = -(-held * batches // 8) * 8
    for at, (b, later) in enumerate(pairs_of(batches)):
        row = pairs_at + at
        payload_ref[row : row + 1, :] = jnp.where(owner_ref[later] == me, weight_ref[b : b + 1, :], 0.0)
    hits = []
    for b in range(batches):
        cell = cells_ref[b : b + 1, :]
        row_hit = (lax.broadcasted_iota(jnp.int32, (tile_rows, nobs), 0) == cell // cols).astype(F32)
        row_hit = row_hit.astype(BF16)
        col_hit = lax.broadcasted_iota(jnp.int32, (cols, nobs), 0) == cell % cols
        hits.append((jnp.concatenate([row_hit] * 3, axis=0), col_hit))
    for tile in range(gx_count):
        fetch(tile).wait()
        put(tile).start()
    folds = cols // nobs
    for slot in range(gx_count):
        for m in range(held):
            for fold in range(folds):
                at = (m * folds + fold) * first
                lanes = slice(fold * nobs, (fold + 1) * nobs)
                pieces[slot][at : at + first, :] = window[row_at ^ slot, m, :first, lanes]
    for b in range(batches):
        row_hit, col_hit = hits[b]
        owner_row = owner_ref[b] // gy_count
        mine = owner_ref[b] % gy_count == col_at
        for m in range(held):
            values = window[owner_row, m]
            high = values.astype(BF16)
            rest = values - high.astype(F32)
            middle, low = split_two(rest)
            stacked = jnp.concatenate([high, middle, low], axis=0)
            columns = lax.dot_general(
                stacked, row_hit, (((0,), (0,)), ((), ())), preferred_element_type=F32
            )
            picked = jnp.sum(jnp.where(col_hit, columns, 0.0), axis=0, keepdims=True)
            row = m * batches + b
            payload_ref[row : row + 1, :] = jnp.where(mine, picked, 0.0)
    for slot in range(gx_count):
        pieces[slot][held * folds * first :, :] = payload_ref[...]
    for tile in range(gx_count):
        put(tile).wait()


def observed_at(owner_ref, cells_ref, b, tile_rows, tile_cols, gy_count, inverse):
    nobs = cells_ref.shape[1]
    cell = cells_ref[b : b + 1, :]
    owner = owner_ref[b]
    ox = ((owner // gy_count) * tile_rows + cell // tile_cols).astype(F32) * inverse
    oy = ((owner % gy_count) * tile_cols + cell % tile_cols).astype(F32) * inverse
    down_x = jnp.transpose(jnp.broadcast_to(ox, (nobs, nobs)))
    down_y = jnp.transpose(jnp.broadcast_to(oy, (nobs, nobs)))
    return ox, oy, down_x, down_y


def tables_body(
    owner_ref, cells_ref, x_ref, y_ref, taper_ref, *, tile_rows, tile_cols, gy_count, inverse
):
    batches, nobs = cells_ref.shape
    left = lax.axis_index("gy") * tile_cols
    places = [
        observed_at(owner_ref, cells_ref, b, tile_rows, tile_cols, gy_count, inverse)
        for b in range(batches)
    ]
    for b, (_, _, down_x, down_y) in enumerate(places):
        x_ref[b] = down_x
        for piece in range(tile_cols // nobs):
            lanes = slice(piece * nobs, (piece + 1) * nobs)
            grid = lax.broadcasted_iota(jnp.int32, (nobs, nobs), 1) + (left + piece * nobs)
            away = down_y - grid.astype(F32) * inverse
            y_ref[b, :, lanes] = away * away
    for at, (b, later) in enumerate(pairs_of(batches)):
        dx = places[b][2] - places[later][0]
        dy = places[b][3] - places[later][1]
        taper_ref[at] = pl.reciprocal(1.0 + (dx * dx + dy * dy))


def once(array):
    return pl.BlockSpec(
        array.shape, lambda i: (0,) * array.ndim, pipeline_mode=pl.Buffered(1)
    )


def merge_body(*refs, base, picks):
    pieces, out_ref = refs[:-1], refs[-1]
    total = None
    for slot, piece in enumerate(pieces):
        out_ref[slot * picks : (slot + 1) * picks, :] = piece[base : base + picks, :]
        weights = piece[base + picks :, :]
        total = weights if total is None else total + weights
    out_ref[len(pieces) * picks :, :] = total


def factor_rows(increment):
    high, low = split_two(increment)
    return jnp.concatenate(
        [jnp.concatenate([high, high], axis=1), jnp.concatenate([low, low], axis=1)], axis=0
    )


def chain_body(
    values_ref, errors_ref, weight_ref, taper_ref, *refs, held, gx_count, gy_count
):
    batches, nobs = values_ref.shape
    members = held * gx_count
    parts, (a_ref, w_ref, prior_ref) = refs[:gy_count], refs[gy_count:]
    row_at = lax.axis_index("gx")
    picks = -(-held * batches // 8) * 8

    def total(first, count):
        rows = [part[first : first + count, :] for part in parts]
        return sum(rows[1:], rows[0])

    for slot in range(gx_count):
        part = total(slot * picks, picks)
        source = held * (row_at ^ slot)
        for m in range(held):
            for b in range(batches):
                row = m * batches + b
                prior_ref[b, pl.ds(source + m, 1), :] = part[row : row + 1, :]
    weights = total(gx_count * picks, parts[0].shape[0] - gx_count * picks)
    for b in range(batches):
        prior = prior_ref[b]
        average = jnp.mean(prior, axis=0, keepdims=True)
        anomaly = prior - average
        spread = jnp.sum(anomaly * anomaly, axis=0, keepdims=True) / (members - 1) + EPSILON
        scaled = anomaly / (spread * (members - 1))
        high, low = split_two(scaled)
        stacked = jnp.concatenate([high, high, low], axis=0).astype(F32)
        wide = a_ref.shape[2]
        if wide > stacked.shape[0]:
            stacked = jnp.concatenate(
                [stacked, jnp.zeros((wide - stacked.shape[0], nobs), F32)], axis=0
            )
        upright = jnp.transpose(stacked).astype(BF16)
        a_ref[b] = upright
        noise = errors_ref[b : b + 1, :]
        post_var = 1.0 / (1.0 / spread + 1.0 / noise)
        post_mean = post_var * (average / spread + values_ref[b : b + 1, :] / noise)
        increment = post_mean - average + (jnp.sqrt(post_var / spread) - 1.0) * anomaly
        w_ref[b] = factor_rows(increment * weight_ref[b : b + 1, :])
        for at, (earlier, later) in enumerate(pairs_of(batches)):
            if earlier != b:
                continue
            there = prior_ref[later]
            deviation = there - jnp.mean(there, axis=0, keepdims=True)
            high, low = split_two(deviation)
            covariance = jnp.dot(
                upright[:, : 3 * members],
                jnp.concatenate([high, low, high], axis=0),
                preferred_element_type=F32,
            )
            high, low = split_two(covariance * taper_ref[at])
            change = jnp.dot(
                factor_rows(increment * weights[at : at + 1, :]),
                jnp.concatenate([high, low], axis=0),
                preferred_element_type=F32,
            )
            prior_ref[later] = there + (change[:members] + change[members:])


def update_body(a_ref, w_ref, x_ref, y_ref, *refs, first, depth, tile_rows, parts, inverse):
    gx_count, ins, outs = parts
    pieces, others, targets = refs[:gx_count], refs[gx_count:ins], refs[ins : ins + outs]
    scratch = refs[-1]
    members, rows, cols = scratch.shape
    held = members // gx_count
    batches, nobs, _ = x_ref.shape
    row_at = lax.axis_index("gx")
    begin = first + pl.program_id(0) * rows
    top = row_at * tile_rows + begin
    from_ref, to_ref = scratch, targets[0]

    def unpack():
        for slot, piece in enumerate(pieces):
            for m in range(held):
                for fold in range(cols // nobs):
                    at = (m * (cols // nobs) + fold) * depth + begin
                    lanes = slice(fold * nobs, (fold + 1) * nobs)
                    from_ref[held * (row_at ^ slot) + m, :, lanes] = piece[
                        pl.ds(pl.multiple_of(at, ROWS), rows), :
                    ]

    if others:
        pl.when(begin < depth)(unpack)

        @pl.when(begin >= depth)
        def _():
            from_ref[...] = others[0][...]
    else:
        unpack()
    if len(targets) > 1:
        to_ref = scratch
    states = [from_ref[:, r, :] for r in range(rows)]
    for b in range(batches):
        scaled = a_ref[b][:, : 3 * members]
        increment = w_ref[b]
        for r in range(rows):
            state = states[r]
            deviation = state - jnp.mean(state, axis=0, keepdims=True)
            high, low = split_two(deviation)
            covariance = jnp.dot(
                scaled, jnp.concatenate([high, low, high], axis=0), preferred_element_type=F32
            )
            dx = x_ref[b] - (top + r).astype(F32) * inverse
            dx = 1.0 + dx * dx
            away = jnp.concatenate([dx] * (cols // nobs), axis=1) + y_ref[b]
            gain = covariance * pl.reciprocal(away)
            high, low = split_two(gain)
            change = jnp.dot(
                increment, jnp.concatenate([high, low], axis=0), preferred_element_type=F32
            )
            states[r] = state + (change[:members] + change[members:])
    for r in range(rows):
        to_ref[:, r, :] = states[r]
    if len(targets) > 1:
        for slot, target in enumerate(targets):
            target[...] = to_ref[pl.ds(held * (row_at ^ slot), held)]


def update(pieces, others, tables, first, count, depth, tile_rows, cols, outs, inverse):
    gx_count = len(pieces)
    batches, nobs, _ = tables[2].shape
    members = tables[1].shape[1] // 2
    rows = count if not others else ROWS
    cells = count * cols * batches * nobs
    out = members // outs
    return pl.pallas_call(
        functools.partial(
            update_body,
            first=first,
            depth=depth,
            tile_rows=tile_rows,
            parts=(gx_count, gx_count + len(others), outs),
            inverse=inverse,
        ),
        grid=(count // rows,),
        in_specs=[once(array) for array in (*tables, *pieces)]
        + [
            pl.BlockSpec(
                (members, rows, cols),
                lambda i: (0, jnp.maximum(i - (depth - first) // rows, 0), 0),
            )
        ]
        * len(others),
        out_specs=[pl.BlockSpec((out, rows, cols), lambda i: (0, i, 0))] * outs,
        out_shape=[jax.ShapeDtypeStruct((out, count, cols), F32)] * outs,
        scratch_shapes=[pltpu.VMEM((members, rows, cols), F32)],
        cost_estimate=pl.CostEstimate(
            flops=cells * members * 10,
            bytes_accessed=8 * members * count * cols,
            transcendentals=cells,
        ),
        compiler_params=LIGHT if others else SPREAD,
        name="update",
    )(*tables, *pieces, *others)


def assemble_body(whole_ref, *refs, first, tile_rows, here):
    pieces, out_ref, sems = refs[:-2], refs[-2], refs[-1]
    row_at = lax.axis_index("gx")
    copies = []
    for tile in range(whole_ref.shape[0]):
        rows = pl.ds(tile * tile_rows, first)
        copies.append(
            pltpu.make_async_copy(whole_ref.at[tile], out_ref.at[:, rows, :], sems.at[tile])
        )
    for slot, piece in enumerate(pieces):
        start = pl.multiple_of((row_at ^ slot) * tile_rows + first, here)
        rows = pl.ds(start, tile_rows - first)
        copies.append(
            pltpu.make_async_copy(
                piece, out_ref.at[:, rows, :], sems.at[whole_ref.shape[0] + slot]
            )
        )
    for copy in copies:
        copy.start()
    for copy in copies:
        copy.wait()


def local(ensemble, obs_values, obs_error, tile_weight, owner_device, obs_cells):
    gx_count = lax.axis_size("gx")
    gy_count = lax.axis_size("gy")
    held, all_rows, tile_cols = ensemble.shape
    members = held * gx_count
    tile_rows = all_rows // gx_count
    batches, nobs = obs_cells.shape
    first = tile_rows * IN_EIGHTHS // 8
    rest = tile_rows - first
    early = tile_rows * OUT_EIGHTHS // 8
    inverse = 1.0 / (all_rows // 4)
    weight = tile_weight[:, :, 0, 0]
    picks, pairs = [-(-n // 8) * 8 for n in (held * batches, len(pairs_of(batches)))]
    payload = picks + pairs
    state_rows = held * (tile_cols // nobs) * first
    in_smem = pl.BlockSpec(memory_space=SMEM)
    in_vmem = pl.BlockSpec(memory_space=VMEM)
    in_hbm = pl.BlockSpec(memory_space=pltpu.MemorySpace.HBM)
    geometry = dict(tile_rows=tile_rows, tile_cols=tile_cols, gy_count=gy_count, inverse=inverse)

    blocks, *pieces = pl.pallas_call(
        functools.partial(
            pick_body, tile_rows=tile_rows, first=first, gx_count=gx_count, gy_count=gy_count
        ),
        in_specs=[in_hbm] * 4,
        out_specs=[in_hbm] + [in_vmem] * gx_count,
        out_shape=[jax.ShapeDtypeStruct((gx_count, held, rest, tile_cols), F32)]
        + [jax.ShapeDtypeStruct((state_rows + payload, nobs), F32)] * gx_count,
        scratch_shapes=[
            pltpu.VMEM((gx_count, held, tile_rows, tile_cols), F32),
            pltpu.VMEM((payload, nobs), F32),
            pltpu.SMEM((batches,), jnp.int32),
            pltpu.VMEM((batches, nobs), jnp.int32),
            pltpu.VMEM((batches, nobs), F32),
            pltpu.SemaphoreType.DMA((gx_count,)),
            pltpu.SemaphoreType.DMA((gx_count,)),
            pltpu.SemaphoreType.DMA((3,)),
        ],
        name="pick",
    )(owner_device, obs_cells, weight, ensemble)
    for slot in range(1, gx_count):
        pieces[slot] = lax.ppermute(pieces[slot], "gx", [(i, i ^ slot) for i in range(gx_count)])
    state = lax.all_to_all(blocks, "gx", split_axis=0, concat_axis=0, tiled=True)
    *places, tapers = pl.pallas_call(
        functools.partial(tables_body, **geometry),
        in_specs=[in_smem, in_vmem],
        out_specs=[in_vmem] * 3,
        out_shape=[
            jax.ShapeDtypeStruct((batches, nobs, nobs), F32),
            jax.ShapeDtypeStruct((batches, nobs, tile_cols), F32),
            jax.ShapeDtypeStruct((len(pairs_of(batches)), nobs, nobs), F32),
        ],
        compiler_params=LIGHT,
        name="tables",
    )(owner_device, obs_cells)
    merge = pl.pallas_call(
        functools.partial(merge_body, base=state_rows, picks=picks),
        in_specs=[in_vmem] * gx_count,
        out_specs=in_vmem,
        out_shape=jax.ShapeDtypeStruct((gx_count * picks + pairs, nobs), F32),
        compiler_params=LIGHT,
        name="merge",
    )
    got = [merge(*pieces)]
    for step in range(1, gy_count):
        got.append(lax.ppermute(got[0], "gy", [(i, i ^ step) for i in range(gy_count)]))
    wide = -(-3 * members // nobs) * nobs
    chain = pl.pallas_call(
        functools.partial(chain_body, held=held, gx_count=gx_count, gy_count=gy_count),
        in_specs=[in_vmem] * (4 + gy_count),
        out_specs=[in_vmem] * 2,
        out_shape=[
            jax.ShapeDtypeStruct((batches, nobs, wide), BF16),
            jax.ShapeDtypeStruct((batches, 2 * members, 2 * nobs), BF16),
        ],
        scratch_shapes=[pltpu.VMEM((batches, members, nobs), F32)],
        compiler_params=LIGHT,
        name="chain",
    )
    factors = chain(obs_values, obs_error, weight, tapers, *got)
    tables = [*factors, *places]

    shape = (first, tile_rows, tile_cols)
    (upper,) = update(pieces, [], tables, 0, early, *shape, 1, inverse)
    upper = lax.all_to_all(
        upper.reshape(gx_count, held, early, tile_cols),
        "gx",
        split_axis=0,
        concat_axis=0,
        tiled=True,
    )
    state = state.reshape(members, rest, tile_cols)
    lower = [
        *update(
            pieces, [state], tables, early, tile_rows - early, *shape, gx_count, inverse
        )
    ]
    for slot in range(1, gx_count):
        lower[slot] = lax.ppermute(
            lower[slot], "gx", [(i, i ^ slot) for i in range(gx_count)]
        )
    return pl.pallas_call(
        functools.partial(assemble_body, first=early, tile_rows=tile_rows, here=ROWS),
        in_specs=[in_vmem] * (1 + gx_count),
        out_specs=in_hbm,
        out_shape=jax.ShapeDtypeStruct(ensemble.shape, F32),
        scratch_shapes=[pltpu.SemaphoreType.DMA((2 * gx_count,))],
        compiler_params=LIGHT,
        name="assemble",
    )(upper, *lower)


def solution(mesh):
    placed = (P("gx", None, "gy"), P(), P(), P(None, None, "gx", "gy"), P(), P())
    return jax.shard_map(
        local, mesh=mesh, in_specs=placed, out_specs=P("gx", None, "gy"), check_vma=False
    )
```
